32 devices in a mesh: groups: 1, seq: 32 (over z, y, x, core).
Axes of the slice: x: 2, y: 2, z: 4, core: 2. Of those that a mesh axis runs over, the one named last changes fastest.
Arguments:
- tokens: bfloat16 [8192, 1024], P(('groups', 'seq')), may hold values from -6 to 6
- values: bfloat16 [8192, 2048], P(('groups', 'seq')), may hold values from -6 to 6
- in_weight: bfloat16 [1024, 288], replicated, may hold values from -0.059814453 to 0.059814453
- step_bias: float32 [32], replicated, may hold values from -4.5 to -3
- decay_log: float32 [32], replicated, may hold values from -9 to 1
- skip_gain: float32 [32], replicated, may hold values from 0.5 to 1.5
- trace_lengths: int32 [4], P('groups'), may hold values from 1 to 4096, 8192 in all
- output_grad: bfloat16 [8192, 2048], P(('groups', 'seq')), may hold values from -6 to 6
Outputs:
- output: bfloat16 [8192, 2048], P(('groups', 'seq'))
- grad_values: bfloat16 [8192, 2048], P(('groups', 'seq'))
- grad_tokens: bfloat16 [8192, 1024], P(('groups', 'seq'))
- grad_in_weight: float32 [1024, 288], P('groups')
- grad_heads: float32 [3, 32], P('groups')
The draws below stay inside these ranges and needn't reach their ends.
Inputs may be any that keep to these rules, and one draw needn't show every extreme that they name: `trace_lengths`: the lengths of the 4 traces packed in order; they sum to 8192 and the longest has exactly 4096 tokens.
All inputs are finite; a program needn't handle non-finite values.
Results may differ from the reference program's by a relative error of at most 0.012.
Values sent between devices are 32-bit elements; how exact they have to be, the bound alone decides.
A program may use at most 320 MiB of HBM per device.

```python
import math
import jax
import jax.numpy as jnp
import numpy as np
from jax import lax

D = 1024
HEADS = 32
STATE = 128
TOK_DEV = 256
TRACES = 4
INNER = 2048
TOKENS = 8192
N_SEQ = 32


def level_of(key, extent, split, least, top_value):
    level, own = 1.0, jax.random.fold_in(key, 6)
    for dim, parts in split:
        draws = jnp.exp(jax.random.uniform(jax.random.fold_in(own, dim), (parts,), jnp.float32, least / len(split), top_value / len(split)))
        level = level * jnp.repeat(draws, extent[dim] // parts).reshape([-1 if axis == dim else 1 for axis in range(len(extent))])
    return level


def length_profile(amount, total, bound, slope):
    weights = [(1 << 20) // math.isqrt(grade ** slope) + 1 for grade in range(2, amount + 1)]
    surplus, holding = total - bound - (amount - 1), [1] * (amount - 1)
    while surplus > 0:
        free = [i for i in range(amount - 1) if holding[i] < bound]
        whole, budget = sum([weights[i] for i in free]), surplus
        for i in free:
            more = min(bound - holding[i], max(1, budget * weights[i] // whole), surplus)
            holding[i] = holding[i] + more
            surplus = surplus - more
    return np.array([bound] + holding)


def ragged_sizes(rng, number_of, total, most, skew):
    if number_of == 2:
        one = jax.random.randint(rng, (), max(1, total - most), min(most, total - 1) + 1)
        return jnp.stack([one, total - one])
    lengths = jnp.asarray(length_profile(number_of, total, most, skew), jnp.int32)
    pairs = (number_of - 1) // 2
    donor, receiver = lengths[1:1 + 2 * pairs:2], lengths[2:2 + 2 * pairs:2]
    slack = jnp.minimum(donor - 1, most - receiver)
    shifted = jax.random.randint(jax.random.fold_in(rng, 1), (pairs,), 0, 1 << 20) % (slack + 1)
    lengths = lengths.at[1:1 + 2 * pairs:2].set(donor - shifted).at[2:2 + 2 * pairs:2].set(receiver + shifted)
    return lengths[jax.random.permutation(jax.random.fold_in(rng, 2), number_of)]


def centred(rng, shape, scale, bound, shards=(), kind=jnp.bfloat16):
    level = level_of(rng, shape, shards, -0.22, 0.18) if shards else 1.0
    values = jax.random.normal(rng, shape, jnp.float32) * scale * level
    return jnp.minimum(jnp.maximum(values, -bound), bound).astype(kind)


def setup_inputs(seed: int = 0, part: int = 0) -> dict:
    seeds = jax.random.split(jax.random.key(seed), 9)
    own_keys = jax.random.split(jax.random.fold_in(seeds[8], part), 9)
    return {
        "tokens": centred(own_keys[0], (TOKENS, D), 1.0, 6.0, ((0, 32),)),
        "values": centred(own_keys[1], (TOKENS, INNER), 1.0, 6.0, ((0, 32),)),
        "in_weight": centred(seeds[2], (D, 2 * STATE + HEADS), 0.01, 0.059814453),
        "step_bias": jnp.clip(jax.random.uniform(seeds[3], (HEADS,), jnp.float32, -4.5, -3.0), -4.5, -3.0),
        "decay_log": jnp.clip(jax.random.uniform(seeds[4], (HEADS,), jnp.float32, -9.0, 1.0), -9.0, 1.0),
        "skip_gain": jnp.clip(jax.random.uniform(seeds[5], (HEADS,), jnp.float32, 0.5, 1.5), 0.5, 1.5),
        "trace_lengths": ragged_sizes(own_keys[6], TRACES, TOKENS, TOKENS // 2, 1).astype(jnp.int32),
        "output_grad": centred(own_keys[7], (TOKENS, INNER), 1.0, 6.0, ((0, 32),)),
    }


def trace_ids(trace_lengths, first_row, count):
    trace_ends = jnp.cumsum(trace_lengths).astype(jnp.int32)
    position = first_row + jnp.arange(count, dtype=jnp.int32)
    return lax.optimization_barrier(jnp.sum((position[:, None] >= trace_ends[None, :]).astype(jnp.int32), axis=1))

def prepare(projected, values, step_bias, decay_log, trace_index, carrying):
    head_count = step_bias.shape[0]
    row_count = values.shape[0]
    head_width = values.shape[1] // head_count
    state_size = (projected.shape[1] - head_count) // 2
    input_map = projected[:, :state_size].astype(jnp.bfloat16)
    output_map = projected[:, state_size:2 * state_size].astype(jnp.bfloat16)
    step_sizes = jax.nn.softplus(projected[:, 2 * state_size:] + step_bias[None, :])
    decays = jnp.cumsum(-jnp.exp(decay_log)[None, :] * step_sizes, axis=0)
    total_decay = decays[-1]
    tail_mask = (trace_index == trace_index[-1]).astype(jnp.float32)
    tail_weight = jnp.exp(total_decay[None, :] - decays) * step_sizes * tail_mask[:, None]
    weighted = (values.reshape(row_count, head_count, head_width).astype(jnp.float32) * tail_weight[:, :, None]).astype(jnp.bfloat16)
    summary = jnp.einsum('lhp,ln->hpn', weighted.astype(jnp.float32), input_map.astype(jnp.float32))
    retained = jnp.exp(total_decay) * carrying[-1]
    return (input_map, output_map, step_sizes, decays, retained, summary)

def head_block(pieces, linked, scores):
    block_decay, block_steps, block_vals = pieces
    group_size = block_decay.shape[0]
    row_count = block_vals.shape[0]
    log_gaps = jnp.where(linked[None] > 0.5, block_decay[:, :, None] - block_decay[:, None, :], 0.0)
    mixing = (jnp.exp(log_gaps) * linked[None] * scores[None] * block_steps[:, None, :]).astype(jnp.bfloat16)
    head_vals = block_vals.reshape(row_count, group_size, -1)
    mixed = jnp.einsum('hij,jhp->ihp', mixing.astype(jnp.float32), head_vals.astype(jnp.float32))
    return mixed.reshape(row_count, -1)

def respond(input_map, output_map, step_sizes, decays, values, skip_gain, incoming, trace_index, carrying):
    head_count = step_sizes.shape[1]
    row_count = values.shape[0]
    head_width = values.shape[1] // head_count
    group_size = min(8, head_count)
    block_count = head_count // group_size
    scores = jnp.dot(output_map, input_map.T, preferred_element_type=jnp.float32)
    position = jnp.arange(row_count, dtype=jnp.int32)
    linked = ((position[:, None] >= position[None, :]) & (trace_index[:, None] == trace_index[None, :])).astype(jnp.float32)
    group_decay = decays.T.reshape(block_count, group_size, row_count)
    group_steps = step_sizes.T.reshape(block_count, group_size, row_count)
    group_vals = values.reshape(row_count, block_count, group_size * head_width).transpose(1, 0, 2)
    kernel = jax.checkpoint(head_block)
    mixed = lax.map(lambda pieces: kernel(pieces, linked, scores), (group_decay, group_steps, group_vals))
    intra = mixed.transpose(1, 0, 2).reshape(row_count, head_count, head_width)
    carried = jnp.einsum('ln,hpn->lhp', output_map.astype(jnp.float32), incoming, precision=lax.Precision.HIGHEST)
    decay_rows = jnp.exp(decays) * carrying[:, None]
    direct = skip_gain[None, :, None] * values.reshape(row_count, head_count, head_width).astype(jnp.float32)
    result = intra + carried * decay_rows[:, :, None] + direct
    return result.reshape(row_count, head_count * head_width)

def reference(tokens, values, in_weight, step_bias, decay_log, skip_gain, trace_lengths, output_grad):
    head_count = step_bias.shape[0]
    inner_width = values.shape[1]
    head_width = inner_width // head_count
    state_size = (in_weight.shape[1] - head_count) // 2
    projected = jnp.dot(tokens, in_weight, preferred_element_type=jnp.float32)

    def forward(projected, values, step_bias, decay_log, skip_gain):

        def advance(carried_state, block_index):
            first_row = (block_index * TOK_DEV).astype(jnp.int32)
            block_proj = lax.dynamic_slice_in_dim(projected, first_row, TOK_DEV, 0)
            block_vals = lax.dynamic_slice_in_dim(values, first_row, TOK_DEV, 0)
            trace_index = trace_ids(trace_lengths, first_row, TOK_DEV)
            prior_trace = trace_ids(trace_lengths, first_row - 1, 1)[0]
            carrying = (trace_index == prior_trace).astype(jnp.float32)
            input_map, output_map, step_sizes, decays, retained, summary = prepare(block_proj, block_vals, step_bias, decay_log, trace_index, carrying)
            block_out = respond(input_map, output_map, step_sizes, decays, block_vals, skip_gain, carried_state, trace_index, carrying)
            return (retained[:, None, None] * carried_state + summary, block_out)
        initial = jnp.zeros((head_count, head_width, state_size), jnp.float32)
        final_state, block_outputs = lax.scan(advance, initial, jnp.arange(N_SEQ, dtype=jnp.int32))
        return block_outputs.reshape(N_SEQ * TOK_DEV, inner_width)
    output_raw, pullback = jax.vjp(forward, projected, values, step_bias, decay_log, skip_gain)
    grad_projected, grad_values, grad_bias, grad_decay, grad_skip = pullback(output_grad.astype(jnp.float32))
    grad_rounded = grad_projected.astype(jnp.bfloat16)
    grad_tokens = jnp.dot(grad_rounded, in_weight.T, preferred_element_type=jnp.float32).astype(jnp.bfloat16)
    grad_in_weight = jnp.dot(tokens.T, grad_rounded, preferred_element_type=jnp.float32)
    grad_heads = jnp.stack([grad_bias, grad_decay, grad_skip])
    return (output_raw.astype(jnp.bfloat16), grad_values, grad_tokens, grad_in_weight, grad_heads)
```

```python
from functools import partial

import jax
import jax.numpy as jnp
from jax import lax
from jax.experimental import pallas as pl
from jax.experimental.pallas import tpu as pltpu
from jax.sharding import PartitionSpec as P


MESH = pl.DeviceIdType.MESH
CORES = 2
CHIPS = 4


def placing(length):
    here = lax.axis_index("seq")
    core = lax.rem(here, CORES)
    chip = lax.rem(lax.div(here, CORES), CHIPS)
    plane = lax.div(here, CORES * CHIPS)
    return core, chip, plane, length // (CORES * CHIPS)


def device_at(plane, chip, core):
    return {"seq": (plane * CHIPS + chip) * CORES + core}


def greet(core, chip, plane, planes):
    barrier = pltpu.get_barrier_semaphore()
    others = [device_at(plane, chip, 1 - core)]
    others += [device_at(plane, lax.rem(chip + d, CHIPS), core) for d in range(1, CHIPS)]
    others += [device_at(lax.rem(plane + d, planes), chip, core) for d in range(1, planes)]
    for other in others:
        pl.semaphore_signal(barrier, inc=1, device_id=other, device_id_type=MESH)
    pl.semaphore_wait(barrier, len(others))


def sending(src, dst, send, recv, at, to):
    return pltpu.make_async_remote_copy(
        src_ref=src,
        dst_ref=dst,
        send_sem=send.at[at],
        recv_sem=recv.at[at],
        device_id=to,
        device_id_type=MESH,
    )


def scan_kernel(length, width, own, out, pair, half, quad, part, zf, zb, gate, back, held, away,
                send, recv, keep):
    core, chip, plane, planes = placing(length)
    greet(core, chip, plane, planes)
    w = width
    heads = own.shape[0]
    mid, low = heads // CORES, heads // (CORES * CHIPS)
    partner = device_at(plane, chip, 1 - core)

    cp = sending(own.at[pl.ds((1 - core) * mid, mid)], pair.at[core], send, recv, 0, partner)
    cp.start()
    mine = pltpu.make_async_copy(own.at[pl.ds(core * mid, mid)], pair.at[core], keep.at[0])
    mine.start()
    mine.wait()
    cp.wait()
    first, second = 0, 1

    def join(h, _):
        f0, r0 = pair[first, h, 0:w], pair[first, h, w : w + 8]
        f1, r1 = pair[second, h, 0:w], pair[second, h, w : w + 8]
        a0, a1 = pair[first, h, w + 8 :], pair[second, h, w + 8 :]
        half[h, 0:w] = f1 + r1[0:1] * f0
        half[h, w : w + 8] = r0 * r1
        half[h, w + 8 :] = a0 + r0[0:1] * a1
        return 0

    lax.fori_loop(0, mid, join, 0)

    copies = []
    for d in range(1, CHIPS):
        to = lax.rem(chip + d, CHIPS)
        cp = sending(
            half.at[pl.ds(to * low, low)], quad.at[chip], send, recv, d, device_at(plane, to, core)
        )
        cp.start()
        copies.append(cp)
    mine = pltpu.make_async_copy(half.at[pl.ds(chip * low, low)], quad.at[chip], keep.at[1])
    mine.start()
    mine.wait()
    for cp in copies:
        cp.wait()

    def total(h, _):
        f, r = quad[0, h, 0:w], quad[0, h, w : w + 8]
        a = quad[CHIPS - 1, h, w + 8 :]
        for c in range(1, CHIPS):
            rc = quad[c, h, w : w + 8]
            f = quad[c, h, 0:w] + rc[0:1] * f
            r = r * rc
            e = CHIPS - 1 - c
            a = quad[e, h, w + 8 :] + quad[e, h, w : w + 1] * a
        part[h, 0:w] = f
        part[h, w : w + 8] = r
        part[h, w + 8 :] = a
        gate[h] = jnp.zeros((2 * w, gate.shape[2]), jnp.float32)
        return 0

    lax.fori_loop(0, low, total, 0)

    base = CHIPS
    ups, downs = [], []
    for d in range(1, planes):
        up = sending(
            part.at[:, 0 : w + 8], zf.at[d - 1], send, recv, base + d,
            device_at(lax.rem(plane + d, planes), chip, core),
        )
        down = sending(
            part.at[:, w : 2 * w + 8], zb.at[d - 1], send, recv, base + planes + d,
            device_at(lax.rem(plane + planes - d, planes), chip, core),
        )
        pl.when(plane + d < planes)(up.start)
        pl.when(plane - d >= 0)(down.start)
        ups.append(up)
        downs.append(down)
    for d in range(planes - 1, 0, -1):

        @pl.when(plane - d >= 0)
        def _():
            ups[d - 1].wait_recv()

            def add(h, _):
                gate[h, 0:w] = zf[d - 1, h, 0:w] + zf[d - 1, h, w : w + 1] * gate[h, 0:w]
                return 0

            lax.fori_loop(0, low, add, 0)

        @pl.when(plane + d < planes)
        def _():
            downs[d - 1].wait_recv()

            def add(h, _):
                gate[h, w:] = zb[d - 1, h, 8:] + zb[d - 1, h, 0:1] * gate[h, w:]
                return 0

            lax.fori_loop(0, low, add, 0)

    def spread(h, _):
        f, a = gate[h, 0:w], gate[h, w:]
        for c in range(CHIPS):
            e = CHIPS - 1 - c
            back[c, h, 0:w] = f
            back[e, h, w:] = a
            if c < CHIPS - 1:
                f = quad[c, h, 0:w] + quad[c, h, w : w + 1] * f
                a = quad[e, h, w + 8 :] + quad[e, h, w : w + 1] * a
        return 0

    lax.fori_loop(0, low, spread, 0)
    base = CHIPS + 2 * planes
    copies = []
    for d in range(1, CHIPS):
        to = lax.rem(chip + d, CHIPS)
        cp = sending(
            back.at[to], held.at[pl.ds(chip * low, low)], send, recv, base + d,
            device_at(plane, to, core),
        )
        cp.start()
        copies.append(cp)
    mine = pltpu.make_async_copy(back.at[chip], held.at[pl.ds(chip * low, low)], keep.at[2])
    mine.start()
    mine.wait()
    for cp in copies:
        cp.wait()

    def last(h, _):
        f, a = held[h, 0:w], held[h, w:]
        f1 = pair[first, h, 0:w] + pair[first, h, w : w + 1] * f
        a0 = pair[second, h, w + 8 :] + pair[second, h, w : w + 1] * a
        early = core == 0
        away[h, 0:w] = jnp.where(early, f1, f)
        away[h, w:] = jnp.where(early, a, a0)
        out[core * mid + h, 0:w] = jnp.where(early, f, f1)
        out[core * mid + h, w:] = jnp.where(early, a0, a)
        return 0

    lax.fori_loop(0, mid, last, 0)
    cp = sending(away, out.at[pl.ds(core * mid, mid)], send, recv, base + CHIPS, partner)
    cp.start()
    for d in range(1, planes):
        pl.when(plane + d < planes)(ups[d - 1].wait_send)
        pl.when(plane - d >= 0)(downs[d - 1].wait_send)
    cp.wait()


def scan_states(summary, seed, retained, length):
    heads, width, state = summary.shape
    gates = jnp.broadcast_to(retained[:, None, None], (heads, 8, state))
    own = jnp.concatenate([summary, gates, seed], axis=1)
    tall = 2 * width + 8
    planes = length // (CORES * CHIPS)
    mid, low = heads // CORES, heads // (CORES * CHIPS)
    count = 2 * CHIPS + 2 * planes + 1
    vmem = lambda *shape: pltpu.VMEM(shape, jnp.float32)
    out = pl.pallas_call(
        partial(scan_kernel, length, width),
        out_shape=jax.ShapeDtypeStruct((heads, 2 * width, state), jnp.float32),
        in_specs=[pl.BlockSpec(memory_space=pltpu.VMEM)],
        out_specs=pl.BlockSpec(memory_space=pltpu.VMEM),
        scratch_shapes=[
            vmem(CORES, mid, tall, state),
            vmem(mid, tall, state),
            vmem(CHIPS, low, tall, state),
            vmem(low, tall, state),
            vmem(planes - 1, low, width + 8, state),
            vmem(planes - 1, low, width + 8, state),
            vmem(low, 2 * width, state),
            vmem(CHIPS, low, 2 * width, state),
            vmem(mid, 2 * width, state),
            vmem(mid, 2 * width, state),
            pltpu.SemaphoreType.DMA((count,)),
            pltpu.SemaphoreType.DMA((count,)),
            pltpu.SemaphoreType.DMA((3,)),
        ],
        compiler_params=pltpu.CompilerParams(
            collective_id=0, has_side_effects=True, vmem_limit_bytes=48 << 20
        ),
    )(own)
    return out[:, :width], out[:, width:]


def sum_kernel(length, own, out, pair, half, quad, part, deep, send, recv):
    core, chip, plane, planes = placing(length)
    greet(core, chip, plane, planes)
    rows = own.shape[0]
    n1, n2, n3 = rows // CORES, rows // (CORES * CHIPS), rows // length
    partner = device_at(plane, chip, 1 - core)

    def across(copies):
        for cp in copies:
            cp.start()
        for cp in copies:
            cp.wait()

    across([sending(own.at[pl.ds((1 - core) * n1, n1)], pair, send, recv, 0, partner)])

    def first(i, _):
        at = pl.multiple_of(i * 64, 64)
        half[pl.ds(at, 64)] = own[pl.ds(core * n1 + at, 64)] + pair[pl.ds(at, 64)]
        return 0

    lax.fori_loop(0, n1 // 64, first, 0)
    chips = [lax.rem(chip + d, CHIPS) for d in range(1, CHIPS)]
    across(
        [
            sending(half.at[pl.ds(to * n2, n2)], quad.at[d], send, recv, 1 + d, device_at(plane, to, core))
            for d, to in enumerate(chips)
        ]
    )

    def second(i, _):
        at = pl.multiple_of(i * 64, 64)
        total = half[pl.ds(chip * n2 + at, 64)]
        for d in range(CHIPS - 1):
            total = total + quad[d, pl.ds(at, 64)]
        part[pl.ds(at, 64)] = total
        return 0

    lax.fori_loop(0, n2 // 64, second, 0)
    others = [lax.rem(plane + d, planes) for d in range(1, planes)]
    across(
        [
            sending(part.at[pl.ds(to * n3, n3)], deep.at[d], send, recv, CHIPS + d, device_at(to, chip, core))
            for d, to in enumerate(others)
        ]
    )
    total = part[pl.ds(plane * n3, n3)]
    for d in range(planes - 1):
        total = total + deep[d]
    at = core * n1 + chip * n2
    out[pl.ds(at + plane * n3, n3)] = total
    base = CHIPS + planes
    block = out.at[pl.ds(at + plane * n3, n3)]
    across(
        [
            sending(block, block, send, recv, base + d, device_at(to, chip, core))
            for d, to in enumerate(others)
        ]
    )
    block = out.at[pl.ds(at, n2)]
    base += planes
    across(
        [
            sending(block, block, send, recv, base + d, device_at(plane, to, core))
            for d, to in enumerate(chips)
        ]
    )
    block = out.at[pl.ds(core * n1, n1)]
    base += CHIPS
    across([sending(block, block, send, recv, base, partner)])


def sum_all(stack, length):
    rows, lanes = stack.shape
    planes = length // (CORES * CHIPS)
    n1, n2, n3 = rows // CORES, rows // (CORES * CHIPS), rows // length
    count = 2 * CHIPS + 2 * planes + 1
    vmem = lambda *shape: pltpu.VMEM(shape, jnp.float32)
    return pl.pallas_call(
        partial(sum_kernel, length),
        out_shape=jax.ShapeDtypeStruct((rows, lanes), jnp.float32),
        in_specs=[pl.BlockSpec(memory_space=pltpu.VMEM)],
        out_specs=pl.BlockSpec(memory_space=pltpu.VMEM),
        scratch_shapes=[
            vmem(n1, lanes),
            vmem(n1, lanes),
            vmem(CHIPS - 1, n2, lanes),
            vmem(n2, lanes),
            vmem(planes - 1, n3, lanes),
            pltpu.SemaphoreType.DMA((count,)),
            pltpu.SemaphoreType.DMA((count,)),
        ],
        compiler_params=pltpu.CompilerParams(
            collective_id=1, has_side_effects=True, vmem_limit_bytes=48 << 20
        ),
    )(stack)


def trace_ids(trace_lengths, first_row, count):
    trace_ends = jnp.cumsum(trace_lengths)
    position = first_row + jnp.arange(count, dtype=jnp.int32)
    return jnp.sum((position[:, None] >= trace_ends[None, :]).astype(jnp.int32), axis=1)


def prepare(projected, values, step_bias, decay_log, trace_index, carrying):
    head_count = step_bias.shape[0]
    row_count = values.shape[0]
    head_width = values.shape[1] // head_count
    state_size = (projected.shape[1] - head_count) // 2
    input_map = projected[:, :state_size].astype(jnp.bfloat16)
    output_map = projected[:, state_size : 2 * state_size].astype(jnp.bfloat16)
    step_sizes = jax.nn.softplus(projected[:, 2 * state_size :] + step_bias[None, :])
    decays = jnp.cumsum(-jnp.exp(decay_log)[None, :] * step_sizes, axis=0)
    total_decay = decays[-1]
    tail_mask = (trace_index == trace_index[-1]).astype(jnp.float32)
    tail_weight = jnp.exp(total_decay[None, :] - decays) * step_sizes * tail_mask[:, None]
    weighted = (values.reshape(row_count, head_count, head_width) * tail_weight[:, :, None]).astype(
        jnp.bfloat16
    )
    summary = jnp.einsum("lhp,ln->hpn", weighted, input_map, preferred_element_type=jnp.float32)
    retained = jnp.exp(total_decay) * carrying[-1]
    return (input_map, output_map, step_sizes, decays, retained, summary)


def head_block(pieces, linked, scores):
    block_decay, block_steps, block_vals = pieces
    group_size = block_decay.shape[0]
    row_count = block_vals.shape[0]
    log_gaps = jnp.where(linked[None] > 0.5, block_decay[:, :, None] - block_decay[:, None, :], 0.0)
    mixing = (jnp.exp(log_gaps) * linked[None] * scores[None] * block_steps[:, None, :]).astype(
        jnp.bfloat16
    )
    head_vals = block_vals.reshape(row_count, group_size, -1)
    mixed = jnp.einsum("hij,jhp->ihp", mixing, head_vals, preferred_element_type=jnp.float32)
    return mixed.reshape(row_count, -1)


def respond(
    input_map,
    output_map,
    step_sizes,
    decays,
    values,
    skip_gain,
    incoming,
    trace_index,
    carrying,
    kernel,
):
    head_count = step_sizes.shape[1]
    row_count = values.shape[0]
    head_width = values.shape[1] // head_count
    group_size = min(8, head_count)
    block_count = head_count // group_size
    scores = jnp.dot(output_map, input_map.T, preferred_element_type=jnp.float32)
    position = jnp.arange(row_count, dtype=jnp.int32)
    linked = (
        (position[:, None] >= position[None, :]) & (trace_index[:, None] == trace_index[None, :])
    ).astype(jnp.float32)
    group_decay = decays.T.reshape(block_count, group_size, row_count)
    group_steps = step_sizes.T.reshape(block_count, group_size, row_count)
    group_vals = values.reshape(row_count, block_count, group_size * head_width).transpose(1, 0, 2)
    mixed = lax.map(
        lambda pieces: kernel(pieces, linked, scores), (group_decay, group_steps, group_vals)
    )
    intra = mixed.transpose(1, 0, 2).reshape(row_count, head_count, head_width)
    carried = jnp.einsum(
        "ln,hpn->lhp", output_map.astype(jnp.float32), incoming, precision=lax.Precision.HIGH
    )
    decay_rows = jnp.exp(decays) * carrying[:, None]
    direct = skip_gain[None, :, None] * values.reshape(row_count, head_count, head_width).astype(
        jnp.float32
    )
    result = intra + carried * decay_rows[:, :, None] + direct
    return result.reshape(row_count, head_count * head_width)


def compose(earlier, later):
    return (earlier[0] * later[0], later[1] + later[0][:, None, None] * earlier[1])


def shards(tokens, values, in_weight, step_bias, decay_log, skip_gain, trace_lengths, output_grad):
    row_count = tokens.shape[0]
    head_count = step_bias.shape[0]
    head_width = values.shape[1] // head_count
    state_size = (in_weight.shape[1] - head_count) // 2
    first_row = lax.axis_index("seq") * row_count
    trace_index = trace_ids(trace_lengths, first_row, row_count)
    prior_trace = trace_ids(trace_lengths, first_row - 1, 1)[0]
    carrying = (trace_index == prior_trace).astype(jnp.float32)
    projected = jnp.dot(tokens, in_weight, preferred_element_type=jnp.float32)
    first_section = partial(prepare, trace_index=trace_index, carrying=carrying)
    (input_map, output_map, step_sizes, decays, retained, summary), pull_first = jax.vjp(
        first_section, projected, values, step_bias, decay_log
    )
    length = lax.axis_size("seq")
    decay_rows = jnp.exp(decays) * carrying[:, None]
    scaled = (
        output_grad.reshape(row_count, head_count, head_width) * decay_rows[:, :, None]
    ).astype(jnp.bfloat16)
    seed = jnp.einsum("lhp,ln->hpn", scaled, output_map, preferred_element_type=jnp.float32)
    incoming, adjoint = scan_states(summary, seed, retained, length)
    kernel = jax.checkpoint(head_block)
    second_section = partial(respond, trace_index=trace_index, carrying=carrying, kernel=kernel)
    output_raw, pull_second = jax.vjp(
        second_section, input_map, output_map, step_sizes, decays, values, skip_gain, incoming
    )
    grads_second = pull_second(output_grad.astype(jnp.float32))
    grad_retained = jnp.sum(adjoint * incoming, axis=(1, 2))
    grads_first = pull_first(
        (grads_second[0], grads_second[1], grads_second[2], grads_second[3], grad_retained, adjoint)
    )
    grad_projected, grad_vals_first, grad_bias, grad_decay = grads_first
    grad_values = grad_vals_first + grads_second[4]
    grad_skip = grads_second[5]
    grad_rounded = grad_projected.astype(jnp.bfloat16)
    grad_tokens = jnp.dot(grad_rounded, in_weight.T, preferred_element_type=jnp.float32).astype(
        jnp.bfloat16
    )
    weight_part = lax.dot_general(
        grad_rounded, tokens, (((0,), (0,)), ((), ())), preferred_element_type=jnp.float32
    )
    columns, width = weight_part.shape
    head_part = jnp.concatenate([grad_bias, grad_decay, grad_skip])
    head_rows = -(-(columns + 1) // 64) * 64 - columns
    head_part = jnp.pad(head_part[None, :], ((0, head_rows - 1), (0, width - 3 * head_count)))
    stack = jnp.concatenate([weight_part, head_part])
    stack = stack.reshape(-1, width // 128, 128).transpose(1, 0, 2).reshape(-1, 128)
    stack = sum_all(stack, length).reshape(width // 128, -1, 128)
    grad_in_weight = stack[:, :columns].transpose(0, 2, 1).reshape(width, columns)
    grad_heads = stack[0, columns, : 3 * head_count].reshape(3, head_count)
    return (output_raw.astype(jnp.bfloat16), grad_values, grad_tokens, grad_in_weight, grad_heads)


def solution(mesh):
    in_specs = (
        P(("groups", "seq"), None),
        P(("groups", "seq"), None),
        P(),
        P(),
        P(),
        P(),
        P("groups"),
        P(("groups", "seq"), None),
    )
    out_specs = (
        P(("groups", "seq"), None),
        P(("groups", "seq"), None),
        P(("groups", "seq"), None),
        P("groups", None),
        P("groups", None),
    )
    return jax.shard_map(shards, mesh=mesh, in_specs=in_specs, out_specs=out_specs, check_vma=False)
```

```python
from functools import partial

import jax
import jax.numpy as jnp
from jax import lax
from jax.experimental import pallas as pl
from jax.experimental.pallas import tpu as pltpu
from jax.sharding import PartitionSpec as P


MESH = pl.DeviceIdType.MESH
CORES = 2
CHIPS = 4


def placing(length):
    here = lax.axis_index("seq")
    core = lax.rem(here, CORES)
    chip = lax.rem(lax.div(here, CORES), CHIPS)
    plane = lax.div(here, CORES * CHIPS)
    return core, chip, plane, length // (CORES * CHIPS)


def device_at(plane, chip, core):
    return {"seq": (plane * CHIPS + chip) * CORES + core}


def greet(length):
    core, chip, plane, planes = placing(length)
    barrier = pltpu.get_barrier_semaphore()
    others = [device_at(plane, chip, 1 - core)]
    others += [device_at(plane, lax.rem(chip + d, CHIPS), core) for d in range(1, CHIPS)]
    others += [device_at(lax.rem(plane + d, planes), chip, core) for d in range(1, planes)]
    for other in others:
        pl.semaphore_signal(barrier, inc=1, device_id=other, device_id_type=MESH)
    return lambda: pl.semaphore_wait(barrier, len(others))


def sending(src, dst, send, recv, at, to):
    return pltpu.make_async_remote_copy(
        src_ref=src,
        dst_ref=dst,
        send_sem=send.at[at],
        recv_sem=recv.at[at],
        device_id=to,
        device_id_type=MESH,
    )


def scan_states(length, width, own, out, pair, half, quad, part, zf, zb, gate, back, held, away,
                send, recv, keep, meanwhile):
    core, chip, plane, planes = placing(length)
    w = width
    heads = own.shape[0]
    mid, low = heads // CORES, heads // (CORES * CHIPS)
    partner = device_at(plane, chip, 1 - core)

    cp = sending(own.at[pl.ds((1 - core) * mid, mid)], pair.at[core], send, recv, 0, partner)
    cp.start()
    mine = pltpu.make_async_copy(own.at[pl.ds(core * mid, mid)], pair.at[core], keep.at[0])
    mine.start()
    mine.wait()
    cp.wait()
    first, second = 0, 1

    def join(h, _):
        f0, r0 = pair[first, h, 0:w], pair[first, h, w : w + 8]
        f1, r1 = pair[second, h, 0:w], pair[second, h, w : w + 8]
        a0, a1 = pair[first, h, w + 8 :], pair[second, h, w + 8 :]
        half[h, 0:w] = f1 + r1[0:1] * f0
        half[h, w : w + 8] = r0 * r1
        half[h, w + 8 :] = a0 + r0[0:1] * a1
        return 0

    lax.fori_loop(0, mid, join, 0)

    copies = []
    for d in range(1, CHIPS):
        to = lax.rem(chip + d, CHIPS)
        cp = sending(
            half.at[pl.ds(to * low, low)], quad.at[chip], send, recv, d, device_at(plane, to, core)
        )
        cp.start()
        copies.append(cp)
    mine = pltpu.make_async_copy(half.at[pl.ds(chip * low, low)], quad.at[chip], keep.at[1])
    mine.start()
    mine.wait()
    meanwhile(0)
    for cp in copies:
        cp.wait()

    def total(h, _):
        f, r = quad[0, h, 0:w], quad[0, h, w : w + 8]
        a = quad[CHIPS - 1, h, w + 8 :]
        for c in range(1, CHIPS):
            rc = quad[c, h, w : w + 8]
            f = quad[c, h, 0:w] + rc[0:1] * f
            r = r * rc
            e = CHIPS - 1 - c
            a = quad[e, h, w + 8 :] + quad[e, h, w : w + 1] * a
        part[h, 0:w] = f
        part[h, w : w + 8] = r
        part[h, w + 8 :] = a
        gate[h] = jnp.zeros((2 * w, gate.shape[2]), jnp.float32)
        return 0

    lax.fori_loop(0, low, total, 0)

    base = CHIPS
    ups, downs = [], []
    for d in range(1, planes):
        up = sending(
            part.at[:, 0 : w + 8], zf.at[d - 1], send, recv, base + d,
            device_at(lax.rem(plane + d, planes), chip, core),
        )
        down = sending(
            part.at[:, w : 2 * w + 8], zb.at[d - 1], send, recv, base + planes + d,
            device_at(lax.rem(plane + planes - d, planes), chip, core),
        )
        pl.when(plane + d < planes)(up.start)
        pl.when(plane - d >= 0)(down.start)
        ups.append(up)
        downs.append(down)
    meanwhile(1)
    for d in range(planes - 1, 0, -1):

        @pl.when(plane - d >= 0)
        def _():
            ups[d - 1].wait_recv()

            def add(h, _):
                gate[h, 0:w] = zf[d - 1, h, 0:w] + zf[d - 1, h, w : w + 1] * gate[h, 0:w]
                return 0

            lax.fori_loop(0, low, add, 0)

        @pl.when(plane + d < planes)
        def _():
            downs[d - 1].wait_recv()

            def add(h, _):
                gate[h, w:] = zb[d - 1, h, 8:] + zb[d - 1, h, 0:1] * gate[h, w:]
                return 0

            lax.fori_loop(0, low, add, 0)

    def spread(h, _):
        f, a = gate[h, 0:w], gate[h, w:]
        for c in range(CHIPS):
            e = CHIPS - 1 - c
            back[c, h, 0:w] = f
            back[e, h, w:] = a
            if c < CHIPS - 1:
                f = quad[c, h, 0:w] + quad[c, h, w : w + 1] * f
                a = quad[e, h, w + 8 :] + quad[e, h, w : w + 1] * a
        return 0

    lax.fori_loop(0, low, spread, 0)
    base = CHIPS + 2 * planes
    copies = []
    for d in range(1, CHIPS):
        to = lax.rem(chip + d, CHIPS)
        cp = sending(
            back.at[to], held.at[pl.ds(chip * low, low)], send, recv, base + d,
            device_at(plane, to, core),
        )
        cp.start()
        copies.append(cp)
    mine = pltpu.make_async_copy(back.at[chip], held.at[pl.ds(chip * low, low)], keep.at[2])
    mine.start()
    mine.wait()
    meanwhile(2)
    for cp in copies:
        cp.wait()

    def last(h, _):
        f, a = held[h, 0:w], held[h, w:]
        f1 = pair[first, h, 0:w] + pair[first, h, w : w + 1] * f
        a0 = pair[second, h, w + 8 :] + pair[second, h, w : w + 1] * a
        early = core == 0
        away[h, 0:w] = jnp.where(early, f1, f)
        away[h, w:] = jnp.where(early, a, a0)
        out[core * mid + h, 0:w] = jnp.where(early, f, f1)
        out[core * mid + h, w:] = jnp.where(early, a0, a)
        return 0

    lax.fori_loop(0, mid, last, 0)
    cp = sending(away, out.at[pl.ds(core * mid, mid)], send, recv, base + CHIPS, partner)
    cp.start()
    for d in range(1, planes):
        pl.when(plane + d < planes)(ups[d - 1].wait_send)
        pl.when(plane - d >= 0)(downs[d - 1].wait_send)
    cp.wait()


def sum_all(length, own, out, pair, half, quad, part, deep, send, recv):
    core, chip, plane, planes = placing(length)
    rows = own.shape[0]
    n1, n2, n3 = rows // CORES, rows // (CORES * CHIPS), rows // length
    partner = device_at(plane, chip, 1 - core)

    def across(copies):
        for cp in copies:
            cp.start()
        for cp in copies:
            cp.wait()

    across([sending(own.at[pl.ds((1 - core) * n1, n1)], pair, send, recv, 0, partner)])

    def first(i, _):
        at = pl.multiple_of(i * 64, 64)
        half[pl.ds(at, 64)] = own[pl.ds(core * n1 + at, 64)] + pair[pl.ds(at, 64)]
        return 0

    lax.fori_loop(0, n1 // 64, first, 0)
    chips = [lax.rem(chip + d, CHIPS) for d in range(1, CHIPS)]
    across(
        [
            sending(half.at[pl.ds(to * n2, n2)], quad.at[d], send, recv, 1 + d, device_at(plane, to, core))
            for d, to in enumerate(chips)
        ]
    )

    def second(i, _):
        at = pl.multiple_of(i * 64, 64)
        total = half[pl.ds(chip * n2 + at, 64)]
        for d in range(CHIPS - 1):
            total = total + quad[d, pl.ds(at, 64)]
        part[pl.ds(at, 64)] = total
        return 0

    lax.fori_loop(0, n2 // 64, second, 0)
    others = [lax.rem(plane + d, planes) for d in range(1, planes)]
    across(
        [
            sending(part.at[pl.ds(to * n3, n3)], deep.at[d], send, recv, CHIPS + d, device_at(to, chip, core))
            for d, to in enumerate(others)
        ]
    )
    total = part[pl.ds(plane * n3, n3)]
    for d in range(planes - 1):
        total = total + deep[d]
    at = core * n1 + chip * n2
    out[pl.ds(at + plane * n3, n3)] = total
    base = CHIPS + planes
    block = out.at[pl.ds(at + plane * n3, n3)]
    across(
        [
            sending(block, block, send, recv, base + d, device_at(to, chip, core))
            for d, to in enumerate(others)
        ]
    )
    block = out.at[pl.ds(at, n2)]
    base += planes
    across(
        [
            sending(block, block, send, recv, base + d, device_at(plane, to, core))
            for d, to in enumerate(chips)
        ]
    )
    block = out.at[pl.ds(core * n1, n1)]
    base += CHIPS
    across([sending(block, block, send, recv, base, partner)])


F32, BF16 = jnp.float32, jnp.bfloat16
LANES = 128
FAR = -1e30


def dot(a, b, dims=((1,), (0,)), precision=None):
    return lax.dot_general(
        a, b, (dims, ((), ())), preferred_element_type=F32, precision=precision
    )


def thirds(x, heads):
    high = x.astype(BF16)
    rest = x - high.astype(F32)
    mid = rest.astype(BF16)
    low = (rest - mid.astype(F32)).astype(BF16)
    keep = [part.astype(F32)[:, :heads] for part in (high, mid, low)]
    keep.append(jnp.zeros((x.shape[0], LANES - 3 * heads), F32))
    return jnp.concatenate(keep, axis=1).astype(BF16)


def layer_kernel(
    length, heads, tokens, values, weight, bias, decay_log, skip_gain, lengths, grad,
    output, grad_values, grad_tokens, total,
    own, states, pair, half, quad, part, zf, zb, gate, back, held, away, send, recv, keep,
    stack, s_pair, s_half, s_quad, s_part, s_deep, s_send, s_recv,
    scores, hidden, grad_scores, mixed, mixed_back, decays3, steps3, rows3, tails3, decays_t,
    b_map, c_map, sums, grad_maps, grad_gate,
):
    ready = greet(length)
    rows, inner = values.shape
    width = inner // heads
    state = (weight.shape[1] - heads) // 2
    pairs = inner // LANES
    per = LANES // width
    here = lax.axis_index("seq")
    first_row = here * rows

    down = lax.broadcasted_iota(jnp.int32, (rows, rows), 0)
    along = lax.broadcasted_iota(jnp.int32, (rows, rows), 1)
    at = first_row + lax.broadcasted_iota(jnp.int32, (rows, 1), 0)
    at_row = first_row + lax.broadcasted_iota(jnp.int32, (1, rows), 1)
    zero = jnp.zeros((rows, 1), jnp.int32)
    trace, trace_row, prior, final = (zero.astype(F32), jnp.zeros((1, rows), F32), zero.astype(F32), zero.astype(F32))
    end = 0
    for k in range(lengths.shape[0]):
        end = end + lengths[k]
        trace += jnp.where(at >= end, 1.0, 0.0)
        trace_row += jnp.where(at_row >= end, 1.0, 0.0)
        prior += jnp.where(zero + (first_row - 1) >= end, 1.0, 0.0)
        final += jnp.where(zero + (first_row + rows - 1) >= end, 1.0, 0.0)
    carrying = jnp.where(trace == prior, 1.0, 0.0)
    tail = jnp.where(trace == final, 1.0, 0.0)
    hidden[...] = jnp.where(down >= along, jnp.where(trace == trace_row, 0.0, FAR), FAR)
    lower = jnp.where(down >= along, 1.0, 0.0).astype(F32)

    projected = dot(tokens[...], weight[...])
    b = projected[:, :state].astype(BF16)
    c = projected[:, state : 2 * state].astype(BF16)
    b_map[...] = b
    c_map[...] = c
    fill = jnp.zeros((1, LANES - heads), F32)
    widen = lambda x: jnp.concatenate([x, jnp.broadcast_to(fill, (x.shape[0], LANES - heads))], axis=1)
    rate = widen(-jnp.exp(decay_log[...]))
    drive = widen(projected[:, 2 * state :] + bias[...])
    steps = jnp.maximum(drive, 0.0) + jnp.log1p(jnp.exp(-jnp.abs(drive)))
    decays = dot(lower, rate * steps, precision=lax.Precision.HIGHEST)
    last = decays[rows - 1 : rows]
    end_gap = jnp.exp(last - decays) * tail
    tails = end_gap * steps
    retained = jnp.exp(last) * carrying[rows - 1 : rows]
    scores[...] = dot(c, b, ((1,), (1,)))
    decays3[...] = thirds(decays, heads)
    steps3[...] = thirds(steps, heads)
    rows3[...] = thirds(jnp.exp(decays) * carrying, heads)
    tails3[...] = thirds(tails, heads)
    decays_t[...] = decays.T
    retained3 = thirds(jnp.broadcast_to(retained, (8, LANES)), heads)
    skip3 = thirds(jnp.broadcast_to(widen(skip_gain[...]), (8, LANES)), heads)
    b_t = b.astype(F32).T.astype(BF16)
    c_t = c.astype(F32).T.astype(BF16)

    up = lax.broadcasted_iota(jnp.int32, (LANES, LANES), 0)
    lane = lax.broadcasted_iota(jnp.int32, (LANES, LANES), 1)

    def spreading(i):
        return jnp.where((up % heads == per * i + lane // width) & (up < 3 * heads), 1.0, 0.0).astype(BF16)

    def columns(i):
        return pl.ds(pl.multiple_of(i * LANES, LANES), LANES)

    def prepare(i, _):
        hot = spreading(i)
        v = values[:, columns(i)].astype(F32)
        g = grad[:, columns(i)].astype(F32)
        w = (v * dot(tails3[...], hot)).astype(BF16)
        u = (g * dot(rows3[...], hot)).astype(BF16)
        own[i, 0:state] = dot(b_t, w)
        own[i, state : state + 8] = dot(retained3, hot)
        own[i, state + 8 :] = dot(c_t, u)
        return 0

    lax.fori_loop(0, pairs, prepare, 0)
    grad_scores[...] = jnp.zeros((rows, rows), F32)
    head_up = lax.broadcasted_iota(jnp.int32, (LANES, rows), 0)
    left = lax.broadcasted_iota(jnp.int32, (1, LANES), 1) // width

    def inside(i, _):
        v = values[:, columns(i)].astype(F32)
        g = grad[:, columns(i)]
        g_t = g.astype(F32).T.astype(BF16)
        scaled = v * dot(steps3[...], spreading(i))
        y = jnp.zeros((rows, LANES), F32)
        zs = []
        for e in range(per):
            h = per * i + e
            hot = jnp.where((head_up % heads == h) & (head_up < 3 * heads), 1.0, 0.0).astype(BF16)
            fade = jnp.exp(dot(decays3[...], hot) - decays_t[pl.ds(h, 1), :] + hidden[...])
            mixing = (scores[...] * fade).astype(BF16)
            one = jnp.where(left == e, scaled, 0.0).astype(BF16)
            grad_scores[...] += dot(g, one, ((1,), (1,))) * fade
            y = y + dot(mixing, one)
            zs.append(dot(g_t[e * width : (e + 1) * width], mixing))
        mixed[:, columns(i)] = y
        mixed_back[:, columns(i)] = jnp.concatenate(zs, axis=0).T
        return 0

    cuts = [0, pairs * 3 // 8, pairs * 6 // 8, pairs]

    def meanwhile(k):
        lax.fori_loop(cuts[k], cuts[k + 1], inside, 0)

    ready()
    scan_states(
        length, state, own, states, pair, half, quad, part, zf, zb, gate, back, held, away,
        send, recv, keep, meanwhile,
    )

    sums[...] = jnp.zeros(sums.shape, F32)
    grad_maps[...] = jnp.zeros(grad_maps.shape, F32)
    grad_gate[...] = jnp.zeros(grad_gate.shape, F32)
    tall = lax.broadcasted_iota(jnp.int32, (2 * LANES, LANES), 0)
    wide = lax.broadcasted_iota(jnp.int32, (2 * LANES, LANES), 1)

    def finish(i, _):
        hot = spreading(i)
        gather = jnp.where(wide == per * i + (tall % LANES) // width, 1.0, 0.0).astype(BF16)

        def by_head(x):
            high = x.astype(BF16)
            low = (x - high.astype(F32)).astype(BF16)
            return dot(jnp.concatenate([high, low], axis=1), gather)

        entering, adjoint = states[i, 0:state], states[i, state:]
        grad_gate[...] += by_head(
            jnp.broadcast_to(jnp.sum(entering * adjoint, axis=0, keepdims=True), (8, LANES))
        )
        entering, adjoint = entering.astype(BF16), adjoint.astype(BF16)
        v = values[:, columns(i)].astype(F32)
        g = grad[:, columns(i)].astype(F32)
        step, row, end = (dot(ref[...], hot) for ref in (steps3, rows3, tails3))
        skip = dot(skip3, hot)[0:1]
        carried = dot(c_map[...], entering) * row
        grad_weighted = dot(b_map[...], adjoint)
        y, z = mixed[:, columns(i)], mixed_back[:, columns(i)]
        weighted = v * end
        output[:, columns(i)] = (y + carried + skip * v).astype(BF16)
        grad_values[:, columns(i)] = (step * z + skip * g + grad_weighted * end).astype(BF16)
        grad_maps[0] += dot(weighted.astype(BF16), adjoint, ((1,), (1,)))
        grad_maps[1] += dot((g * row).astype(BF16), entering, ((1,), (1,)))
        scaled = (v * step).astype(BF16).astype(F32)
        sums[0] += by_head(g * (y + carried) - scaled * z - weighted * grad_weighted)
        sums[1] += by_head(v * z)
        sums[2] += by_head(v * grad_weighted)
        sums[3] += by_head(g * v)
        return 0

    lax.fori_loop(0, pairs, finish, 0)
    through = sums[2]
    grad_last = jnp.sum(tails * through, axis=0, keepdims=True) + retained * grad_gate[0:1]
    grad_rates = dot(lower, sums[0], ((0,), (0,)), lax.Precision.HIGHEST) + grad_last
    grad_steps = sums[1] + end_gap * through + rate * grad_rates
    grad_drive = grad_steps * jax.nn.sigmoid(drive)
    grad_s = grad_scores[...]
    grad_b = grad_maps[0] + dot(grad_s.T.astype(BF16), c)
    grad_c = grad_maps[1] + dot(grad_s.astype(BF16), b)
    grad_maps_b = jnp.concatenate([grad_b, grad_c], axis=1)
    rounded = grad_maps_b.astype(BF16)
    rounded_drive = grad_drive[:, :heads].astype(BF16)
    split = 2 * state
    flipped = jnp.concatenate([grad_maps_b.T, grad_drive.T[:heads]], axis=0).astype(BF16)
    blocks = tokens.shape[1] // LANES
    high, used = stack.shape[0] // blocks, split + heads
    for k in range(blocks):
        base = k * high
        stack[base : base + used] = dot(flipped, tokens[:, k * LANES : (k + 1) * LANES])
        stack[base + used : base + high] = jnp.zeros((high - used, LANES), F32)
    stack[used : used + 1] = jnp.sum(grad_drive, axis=0, keepdims=True)
    stack[used + 1 : used + 2] = rate * jnp.sum(
        grad_rates * steps, axis=0, keepdims=True
    )
    stack[used + 2 : used + 3] = jnp.sum(sums[3], axis=0, keepdims=True)

    grad_tokens[...] = (
        dot(rounded, weight[:, :split], ((1,), (1,)))
        + dot(rounded_drive, weight[:, split:], ((1,), (1,)))
    ).astype(BF16)
    sum_all(length, stack, total, s_pair, s_half, s_quad, s_part, s_deep, s_send, s_recv)


def shards(tokens, values, in_weight, step_bias, decay_log, skip_gain, trace_lengths, output_grad):
    row_count, inner = values.shape
    depth = tokens.shape[1]
    head_count = step_bias.shape[0]
    columns = in_weight.shape[1]
    state = (columns - head_count) // 2
    length = lax.axis_size("seq")
    planes = length // (CORES * CHIPS)
    pairs = inner // LANES
    mid, low = pairs // CORES, pairs // (CORES * CHIPS)
    tall = 2 * state + 8
    blocks = depth // LANES
    high = -(-(columns + 3) // 64) * 64
    lines = blocks * high
    n1, n2, n3 = lines // CORES, lines // (CORES * CHIPS), lines // length
    vmem = lambda *shape: pltpu.VMEM(shape, F32)
    half = lambda *shape: pltpu.VMEM(shape, BF16)
    here = pl.BlockSpec(memory_space=pltpu.VMEM)
    count = 2 * CHIPS + 2 * planes + 1
    output, grad_values, grad_tokens, total = pl.pallas_call(
        partial(layer_kernel, length, head_count),
        out_shape=(
            jax.ShapeDtypeStruct(values.shape, BF16),
            jax.ShapeDtypeStruct(values.shape, BF16),
            jax.ShapeDtypeStruct(tokens.shape, BF16),
            jax.ShapeDtypeStruct((lines, LANES), F32),
        ),
        in_specs=[here] * 6 + [pl.BlockSpec(memory_space=pltpu.SMEM), here],
        out_specs=(here,) * 4,
        scratch_shapes=[
            vmem(pairs, tall, LANES),
            vmem(pairs, 2 * state, LANES),
            vmem(CORES, mid, tall, LANES),
            vmem(mid, tall, LANES),
            vmem(CHIPS, low, tall, LANES),
            vmem(low, tall, LANES),
            vmem(planes - 1, low, state + 8, LANES),
            vmem(planes - 1, low, state + 8, LANES),
            vmem(low, 2 * state, LANES),
            vmem(CHIPS, low, 2 * state, LANES),
            vmem(mid, 2 * state, LANES),
            vmem(mid, 2 * state, LANES),
            pltpu.SemaphoreType.DMA((count,)),
            pltpu.SemaphoreType.DMA((count,)),
            pltpu.SemaphoreType.DMA((3,)),
            vmem(lines, LANES),
            vmem(n1, LANES),
            vmem(n1, LANES),
            vmem(CHIPS - 1, n2, LANES),
            vmem(n2, LANES),
            vmem(planes - 1, n3, LANES),
            pltpu.SemaphoreType.DMA((count,)),
            pltpu.SemaphoreType.DMA((count,)),
            vmem(row_count, row_count),
            vmem(row_count, row_count),
            vmem(row_count, row_count),
            vmem(row_count, inner),
            vmem(row_count, inner),
            half(row_count, LANES),
            half(row_count, LANES),
            half(row_count, LANES),
            half(row_count, LANES),
            vmem(LANES, row_count),
            half(row_count, state),
            half(row_count, state),
            vmem(4, row_count, LANES),
            vmem(2, row_count, state),
            vmem(8, LANES),
        ],
        compiler_params=pltpu.CompilerParams(
            collective_id=0, has_side_effects=True, vmem_limit_bytes=56 << 20
        ),
    )(
        tokens, values, in_weight, step_bias[None], decay_log[None], skip_gain[None],
        trace_lengths, output_grad,
    )
    total = total.reshape(blocks, high, LANES)
    grad_in_weight = total[:, :columns].transpose(0, 2, 1).reshape(depth, columns)
    grad_heads = total[0, columns : columns + 3, :head_count]
    return output, grad_values, grad_tokens, grad_in_weight, grad_heads


def solution(mesh):
    in_specs = (
        P(("groups", "seq"), None),
        P(("groups", "seq"), None),
        P(),
        P(),
        P(),
        P(),
        P("groups"),
        P(("groups", "seq"), None),
    )
    out_specs = (
        P(("groups", "seq"), None),
        P(("groups", "seq"), None),
        P(("groups", "seq"), None),
        P("groups", None),
        P("groups", None),
    )
    return jax.shard_map(shards, mesh=mesh, in_specs=in_specs, out_specs=out_specs, check_vma=False)
```

```python
from functools import partial

import jax
import jax.numpy as jnp
from jax import lax
from jax.experimental import pallas as pl
from jax.experimental.pallas import tpu as pltpu
from jax.sharding import PartitionSpec as P


MESH = pl.DeviceIdType.MESH
CORES = 2
CHIPS = 4


def placing(length):
    here = lax.axis_index("seq")
    core = lax.rem(here, CORES)
    chip = lax.rem(lax.div(here, CORES), CHIPS)
    plane = lax.div(here, CORES * CHIPS)
    return core, chip, plane, length // (CORES * CHIPS)


def device_at(plane, chip, core):
    return {"seq": (plane * CHIPS + chip) * CORES + core}


def greet(length):
    core, chip, plane, planes = placing(length)
    barrier = pltpu.get_barrier_semaphore()
    others = [device_at(plane, chip, 1 - core)]
    others += [device_at(plane, lax.rem(chip + d, CHIPS), core) for d in range(1, CHIPS)]
    others += [device_at(lax.rem(plane + d, planes), chip, core) for d in range(1, planes)]
    for other in others:
        pl.semaphore_signal(barrier, inc=1, device_id=other, device_id_type=MESH)
    return lambda: pl.semaphore_wait(barrier, len(others))


def sending(src, dst, send, recv, at, to):
    return pltpu.make_async_remote_copy(
        src_ref=src,
        dst_ref=dst,
        send_sem=send.at[at],
        recv_sem=recv.at[at],
        device_id=to,
        device_id_type=MESH,
    )


def scan_stream(width, places, own, out, pair, half, quad, part, zf, zb, gate, back, held, away,
                send, recv, keep):
    core, chip, plane, planes = places
    w = width
    heads = own.shape[0]
    mid, low = heads // CORES, heads // (CORES * CHIPS)
    partner = device_at(plane, chip, 1 - core)
    pending = []

    def begin(cp):
        cp.start()
        pending.append(cp)

    def settle():
        for cp in pending:
            cp.wait()
        pending.clear()

    begin(sending(own.at[pl.ds((1 - core) * mid, mid)], pair.at[core], send, recv, 0, partner))
    yield
    mine = pltpu.make_async_copy(own.at[pl.ds(core * mid, mid)], pair.at[core], keep.at[0])
    mine.start()
    mine.wait()
    yield
    settle()

    def join(h, _):
        r0, r1 = pair[0, h, w : w + 8], pair[1, h, w : w + 8]
        half[h, 0:w] = pair[1, h, 0:w] + r1[0:1] * pair[0, h, 0:w]
        half[h, w : w + 8] = r0 * r1
        half[h, w + 8 :] = pair[0, h, w + 8 :] + r0[0:1] * pair[1, h, w + 8 :]
        return 0

    lax.fori_loop(0, mid, join, 0)
    chips = [lax.rem(chip + d, CHIPS) for d in range(1, CHIPS)]
    for d, to in enumerate(chips):
        begin(
            sending(
                half.at[pl.ds(to * low, low)], quad.at[chip], send, recv, 1 + d,
                device_at(plane, to, core),
            )
        )
    mine = pltpu.make_async_copy(half.at[pl.ds(chip * low, low)], quad.at[chip], keep.at[1])
    mine.start()
    mine.wait()
    yield
    settle()

    def total(h, _):
        f, r = quad[0, h, 0:w], quad[0, h, w : w + 8]
        a = quad[CHIPS - 1, h, w + 8 :]
        for c in range(1, CHIPS):
            rc = quad[c, h, w : w + 8]
            f = quad[c, h, 0:w] + rc[0:1] * f
            r = r * rc
            e = CHIPS - 1 - c
            a = quad[e, h, w + 8 :] + quad[e, h, w : w + 1] * a
        part[h, 0:w] = f
        part[h, w : w + 8] = r
        part[h, w + 8 :] = a
        gate[h] = jnp.zeros((2 * w, gate.shape[2]), jnp.float32)
        return 0

    lax.fori_loop(0, low, total, 0)
    ups, downs = [], []
    for d in range(1, planes):
        up = sending(
            part.at[:, 0 : w + 8], zf.at[d - 1], send, recv, CHIPS + d,
            device_at(lax.rem(plane + d, planes), chip, core),
        )
        down = sending(
            part.at[:, w : 2 * w + 8], zb.at[d - 1], send, recv, CHIPS + planes + d,
            device_at(lax.rem(plane + planes - d, planes), chip, core),
        )
        pl.when(plane + d < planes)(up.start)
        pl.when(plane - d >= 0)(down.start)
        ups.append(up)
        downs.append(down)
    yield
    for d in range(planes - 1, 0, -1):

        @pl.when(plane - d >= 0)
        def _():
            ups[d - 1].wait_recv()

            def add(h, _):
                gate[h, 0:w] = zf[d - 1, h, 0:w] + zf[d - 1, h, w : w + 1] * gate[h, 0:w]
                return 0

            lax.fori_loop(0, low, add, 0)

        @pl.when(plane + d < planes)
        def _():
            downs[d - 1].wait_recv()

            def add(h, _):
                gate[h, w:] = zb[d - 1, h, 8:] + zb[d - 1, h, 0:1] * gate[h, w:]
                return 0

            lax.fori_loop(0, low, add, 0)

    def spread(h, _):
        f, a = gate[h, 0:w], gate[h, w:]
        for c in range(CHIPS):
            e = CHIPS - 1 - c
            back[c, h, 0:w] = f
            back[e, h, w:] = a
            if c < CHIPS - 1:
                f = quad[c, h, 0:w] + quad[c, h, w : w + 1] * f
                a = quad[e, h, w + 8 :] + quad[e, h, w : w + 1] * a
        return 0

    lax.fori_loop(0, low, spread, 0)
    base = CHIPS + 2 * planes
    for d, to in enumerate(chips):
        begin(
            sending(
                back.at[to], held.at[pl.ds(chip * low, low)], send, recv, base + d,
                device_at(plane, to, core),
            )
        )
    mine = pltpu.make_async_copy(back.at[chip], held.at[pl.ds(chip * low, low)], keep.at[2])
    mine.start()
    mine.wait()
    yield
    settle()

    def last(h, _):
        f, a = held[h, 0:w], held[h, w:]
        f1 = pair[0, h, 0:w] + pair[0, h, w : w + 1] * f
        a0 = pair[1, h, w + 8 :] + pair[1, h, w : w + 1] * a
        early = core == 0
        away[h, 0:w] = jnp.where(early, f1, f)
        away[h, w:] = jnp.where(early, a, a0)
        out[core * mid + h, 0:w] = jnp.where(early, f, f1)
        out[core * mid + h, w:] = jnp.where(early, a0, a)
        return 0

    lax.fori_loop(0, mid, last, 0)
    begin(sending(away, out.at[pl.ds((core) * mid, mid)], send, recv, base + CHIPS, partner))
    for d in range(1, planes):
        pl.when(plane + d < planes)(ups[d - 1].wait_send)
        pl.when(plane - d >= 0)(downs[d - 1].wait_send)
    yield
    settle()
    yield


def sum_stream(length, places, own, out, pair, half, quad, part, deep, send, recv):
    core, chip, plane, planes = places
    rows = own.shape[0]
    n1, n2, n3 = rows // CORES, rows // (CORES * CHIPS), rows // length
    partner = device_at(plane, chip, 1 - core)
    pending = []

    def begin(src, dst, at, to):
        cp = sending(src, dst, send, recv, at, to)
        cp.start()
        pending.append(cp)

    def settle():
        for cp in pending:
            cp.wait()
        pending.clear()

    begin(own.at[pl.ds((1 - core) * n1, n1)], pair, 0, partner)
    yield
    settle()
    half[...] = own[pl.ds(core * n1, n1)] + pair[...]
    chips = [lax.rem(chip + d, CHIPS) for d in range(1, CHIPS)]
    for d, to in enumerate(chips):
        begin(half.at[pl.ds(to * n2, n2)], quad.at[d], 1 + d, device_at(plane, to, core))
    yield
    settle()
    summed = half[pl.ds(chip * n2, n2)]
    for d in range(CHIPS - 1):
        summed = summed + quad[d]
    part[...] = summed
    others = [lax.rem(plane + d, planes) for d in range(1, planes)]
    for d, to in enumerate(others):
        begin(part.at[pl.ds(to * n3, n3)], deep.at[d], CHIPS + d, device_at(to, chip, core))
    yield
    settle()
    summed = part[pl.ds(plane * n3, n3)]
    for d in range(planes - 1):
        summed = summed + deep[d]
    at = core * n1 + chip * n2
    out[pl.ds(at + plane * n3, n3)] = summed
    base = CHIPS + planes
    block = out.at[pl.ds(at + plane * n3, n3)]
    for d, to in enumerate(others):
        begin(block, block, base + d, device_at(to, chip, core))
    yield
    settle()
    block = out.at[pl.ds(at, n2)]
    base += planes
    for d, to in enumerate(chips):
        begin(block, block, base + d, device_at(plane, to, core))
    yield
    settle()
    block = out.at[pl.ds(core * n1, n1)]
    begin(block, block, base + CHIPS, partner)
    yield
    settle()
    yield


F32, BF16 = jnp.float32, jnp.bfloat16
LANES = 128
FAR = -1e30
STREAMS = 2
SHARES = ((2, 3), (2, 3), (2, 4))


def dot(a, b, dims=((1,), (0,)), precision=None):
    return lax.dot_general(
        a, b, (dims, ((), ())), preferred_element_type=F32, precision=precision
    )


def thirds(x, heads):
    high = x.astype(BF16)
    rest = x - high.astype(F32)
    mid = rest.astype(BF16)
    low = (rest - mid.astype(F32)).astype(BF16)
    keep = [part.astype(F32)[:, :heads] for part in (high, mid, low)]
    keep.append(jnp.zeros((x.shape[0], LANES - 3 * heads), F32))
    return jnp.concatenate(keep, axis=1).astype(BF16)


def layer_kernel(
    length, heads, tokens, values, weight, bias, decay_log, skip_gain, lengths, grad,
    output, grad_values, grad_tokens, grad_weight, grad_heads,
    own, states, pair, half, quad, part, zf, zb, gate, back, held, away, send, recv, keep,
    stack, total, s_pair, s_half, s_quad, s_part, s_deep, s_send, s_recv,
    scores, hidden, grad_scores, mixed, mixed_back, decays3, steps3, rows3, tails3, decays_t,
    b_map, c_map, sums, grad_maps, grad_gate,
):
    ready = greet(length)
    rows, inner = values.shape
    width = inner // heads
    state = (weight.shape[0] - heads) // 2
    pairs = inner // LANES
    per = LANES // width
    here = lax.axis_index("seq")
    first_row = here * rows

    down = lax.broadcasted_iota(jnp.int32, (rows, rows), 0)
    along = lax.broadcasted_iota(jnp.int32, (rows, rows), 1)
    at = first_row + lax.broadcasted_iota(jnp.int32, (rows, 1), 0)
    at_row = first_row + lax.broadcasted_iota(jnp.int32, (1, rows), 1)
    zero = jnp.zeros((rows, 1), jnp.int32)
    trace, trace_row, prior, final = (zero.astype(F32), jnp.zeros((1, rows), F32), zero.astype(F32), zero.astype(F32))
    end = 0
    for k in range(lengths.shape[0]):
        end = end + lengths[k]
        trace += jnp.where(at >= end, 1.0, 0.0)
        trace_row += jnp.where(at_row >= end, 1.0, 0.0)
        prior += jnp.where(zero + (first_row - 1) >= end, 1.0, 0.0)
        final += jnp.where(zero + (first_row + rows - 1) >= end, 1.0, 0.0)
    carrying = jnp.where(trace == prior, 1.0, 0.0)
    tail = jnp.where(trace == final, 1.0, 0.0)
    hidden[...] = jnp.where(down >= along, jnp.where(trace == trace_row, 0.0, FAR), FAR)
    lower = jnp.where(down >= along, 1.0, 0.0).astype(F32)

    projected = dot(tokens[...], weight[...], ((1,), (1,)))
    b = projected[:, :state].astype(BF16)
    c = projected[:, state : 2 * state].astype(BF16)
    b_map[...] = b
    c_map[...] = c
    fill = jnp.zeros((1, LANES - heads), F32)
    widen = lambda x: jnp.concatenate([x, jnp.broadcast_to(fill, (x.shape[0], LANES - heads))], axis=1)
    rate = widen(-jnp.exp(decay_log[...]))
    drive = widen(projected[:, 2 * state :] + bias[...])
    steps = jnp.maximum(drive, 0.0) + jnp.log1p(jnp.exp(-jnp.abs(drive)))
    decays = dot(lower, rate * steps, precision=lax.Precision.HIGHEST)
    last = decays[rows - 1 : rows]
    end_gap = jnp.exp(last - decays) * tail
    tails = end_gap * steps
    retained = jnp.exp(last) * carrying[rows - 1 : rows]
    scores[...] = dot(c, b, ((1,), (1,)))
    decays3[...] = thirds(decays, heads)
    steps3[...] = thirds(steps, heads)
    rows3[...] = thirds(jnp.exp(decays) * carrying, heads)
    tails3[...] = thirds(tails, heads)
    decays_t[...] = decays.T
    retained3 = thirds(jnp.broadcast_to(retained, (8, LANES)), heads)
    skip3 = thirds(jnp.broadcast_to(widen(skip_gain[...]), (8, LANES)), heads)
    b_t = b.astype(F32).T.astype(BF16)
    c_t = c.astype(F32).T.astype(BF16)

    up = lax.broadcasted_iota(jnp.int32, (LANES, LANES), 0)
    lane = lax.broadcasted_iota(jnp.int32, (LANES, LANES), 1)

    def spreading(i):
        return jnp.where((up % heads == per * i + lane // width) & (up < 3 * heads), 1.0, 0.0).astype(BF16)

    def columns(i):
        return pl.ds(pl.multiple_of(i * LANES, LANES), LANES)

    def prepare(i, _):
        hot = spreading(i)
        v = values[:, columns(i)].astype(F32)
        g = grad[:, columns(i)].astype(F32)
        w = (v * dot(tails3[...], hot)).astype(BF16)
        u = (g * dot(rows3[...], hot)).astype(BF16)
        own[i, 0:state] = dot(b_t, w)
        own[i, state : state + 8] = dot(retained3, hot)
        own[i, state + 8 :] = dot(c_t, u)
        return 0

    grad_scores[...] = jnp.zeros((rows, rows), F32)
    head_up = lax.broadcasted_iota(jnp.int32, (LANES, rows), 0)
    left = lax.broadcasted_iota(jnp.int32, (1, LANES), 1) // width

    def inside(i, _):
        v = values[:, columns(i)].astype(F32)
        g = grad[:, columns(i)]
        g_t = g.astype(F32).T.astype(BF16)
        scaled = v * dot(steps3[...], spreading(i))
        y = jnp.zeros((rows, LANES), F32)
        zs = []
        for e in range(per):
            h = per * i + e
            hot = jnp.where((head_up % heads == h) & (head_up < 3 * heads), 1.0, 0.0).astype(BF16)
            fade = jnp.exp(dot(decays3[...], hot) - decays_t[pl.ds(h, 1), :] + hidden[...])
            mixing = (scores[...] * fade).astype(BF16)
            one = jnp.where(left == e, scaled, 0.0).astype(BF16)
            grad_scores[...] += dot(g, one, ((1,), (1,))) * fade
            y = y + dot(mixing, one)
            zs.append(dot(g_t[e * width : (e + 1) * width], mixing))
        mixed[:, columns(i)] = y
        mixed_back[:, columns(i)] = jnp.concatenate(zs, axis=0).T
        return 0

    places = placing(length)
    core = places[0]
    chunk = pairs // STREAMS
    mid = chunk // CORES
    done = 0

    def meanwhile(amount):
        nonlocal done
        upto = min(pairs, done + amount)
        lax.fori_loop(done, upto, inside, 0)
        done = upto

    streams = [
        scan_stream(
            state, places, own.at[pl.ds(q * chunk, chunk)], states.at[pl.ds(q * chunk, chunk)],
            *(ref.at[q] for ref in (pair, half, quad, part, zf, zb, gate, back, held, away)),
            send.at[q], recv.at[q], keep.at[q],
        )
        for q in range(STREAMS)
    ]
    for q in range(STREAMS):
        theirs = q * chunk + (1 - core) * mid
        lax.fori_loop(0, mid, lambda h, _: prepare(theirs + h, 0), 0)
        if q == 0:
            ready()
        next(streams[q])
        ours = q * chunk + core * mid
        lax.fori_loop(0, mid, lambda h, _: prepare(ours + h, 0), 0)
        next(streams[q])
    for shares in SHARES:
        for q in range(STREAMS):
            next(streams[q])
            meanwhile(shares[q] * pairs // 16)
    meanwhile(pairs)
    for q in range(STREAMS):
        next(streams[q])

    sums[...] = jnp.zeros(sums.shape, F32)
    grad_maps[...] = jnp.zeros(grad_maps.shape, F32)
    grad_gate[...] = jnp.zeros(grad_gate.shape, F32)
    tall = lax.broadcasted_iota(jnp.int32, (2 * LANES, LANES), 0)
    wide = lax.broadcasted_iota(jnp.int32, (2 * LANES, LANES), 1)

    def finish(i, _):
        hot = spreading(i)
        gather = jnp.where(wide == per * i + (tall % LANES) // width, 1.0, 0.0).astype(BF16)

        def by_head(x):
            high = x.astype(BF16)
            low = (x - high.astype(F32)).astype(BF16)
            return dot(jnp.concatenate([high, low], axis=1), gather)

        entering, adjoint = states[i, 0:state], states[i, state:]
        grad_gate[...] += by_head(
            jnp.broadcast_to(jnp.sum(entering * adjoint, axis=0, keepdims=True), (8, LANES))
        )
        entering, adjoint = entering.astype(BF16), adjoint.astype(BF16)
        v = values[:, columns(i)].astype(F32)
        g = grad[:, columns(i)].astype(F32)
        step, row, end = (dot(ref[...], hot) for ref in (steps3, rows3, tails3))
        skip = dot(skip3, hot)[0:1]
        carried = dot(c_map[...], entering) * row
        grad_weighted = dot(b_map[...], adjoint)
        y, z = mixed[:, columns(i)], mixed_back[:, columns(i)]
        weighted = v * end
        output[:, columns(i)] = (y + carried + skip * v).astype(BF16)
        grad_values[:, columns(i)] = (step * z + skip * g + grad_weighted * end).astype(BF16)
        grad_maps[0] += dot(weighted.astype(BF16), adjoint, ((1,), (1,)))
        grad_maps[1] += dot((g * row).astype(BF16), entering, ((1,), (1,)))
        scaled = (v * step).astype(BF16).astype(F32)
        sums[0] += by_head(g * (y + carried) - scaled * z - weighted * grad_weighted)
        sums[1] += by_head(v * z)
        sums[2] += by_head(v * grad_weighted)
        sums[3] += by_head(g * v)
        return 0

    for q in range(STREAMS):
        ours = q * chunk + core * mid
        lax.fori_loop(0, mid, lambda h, _: finish(ours + h, 0), 0)
        next(streams[q])
        theirs = q * chunk + (1 - core) * mid
        lax.fori_loop(0, mid, lambda h, _: finish(theirs + h, 0), 0)
    through = sums[2]
    grad_last = jnp.sum(tails * through, axis=0, keepdims=True) + retained * grad_gate[0:1]
    grad_rates = dot(lower, sums[0], ((0,), (0,)), lax.Precision.HIGHEST) + grad_last
    grad_steps = sums[1] + end_gap * through + rate * grad_rates
    grad_drive = grad_steps * jax.nn.sigmoid(drive)
    grad_s = grad_scores[...]
    grad_b = grad_maps[0] + dot(grad_s.T.astype(BF16), c)
    grad_c = grad_maps[1] + dot(grad_s.astype(BF16), b)
    grad_maps_b = jnp.concatenate([grad_b, grad_c], axis=1)
    rounded = grad_maps_b.astype(BF16)
    rounded_drive = grad_drive[:, :heads].astype(BF16)
    split = 2 * state
    flipped = jnp.concatenate([grad_maps_b.T, grad_drive.T[:heads]], axis=0).astype(BF16)
    blocks = tokens.shape[1] // LANES
    high, used = stack.shape[0] // blocks, split + heads
    for k in range(blocks):
        base = k * high
        stack[base : base + used] = dot(flipped, tokens[:, k * LANES : (k + 1) * LANES])
        stack[base + used : base + high] = jnp.zeros((high - used, LANES), F32)
    stack[used : used + 1] = jnp.sum(grad_drive, axis=0, keepdims=True)
    stack[used + 1 : used + 2] = rate * jnp.sum(
        grad_rates * steps, axis=0, keepdims=True
    )
    stack[used + 2 : used + 3] = jnp.sum(sums[3], axis=0, keepdims=True)

    split_rows = stack.shape[0] // s_pair.shape[0]
    streams = [
        sum_stream(
            length, places, stack.at[pl.ds(q * split_rows, split_rows)],
            total.at[pl.ds(q * split_rows, split_rows)],
            *(ref.at[q] for ref in (s_pair, s_half, s_quad, s_part, s_deep, s_send, s_recv)),
        )
        for q in range(s_pair.shape[0])
    ]
    for stream in streams:
        next(stream)
    grad_tokens[...] = (
        dot(rounded, weight[:split])
        + dot(rounded_drive, weight[split:])
    ).astype(BF16)
    for _ in range(6):
        for stream in streams:
            next(stream)
    for k in range(blocks):
        grad_weight[:, k * LANES : (k + 1) * LANES] = total[k * high : k * high + used]
    grad_heads[...] = total[used : used + 8]


def shards(tokens, values, in_weight, step_bias, decay_log, skip_gain, trace_lengths, output_grad):
    row_count, inner = values.shape
    depth = tokens.shape[1]
    head_count = step_bias.shape[0]
    columns = in_weight.shape[1]
    state = (columns - head_count) // 2
    length = lax.axis_size("seq")
    planes = length // (CORES * CHIPS)
    pairs = inner // LANES
    chunk = pairs // STREAMS
    mid, low = chunk // CORES, chunk // (CORES * CHIPS)
    tall = 2 * state + 8
    blocks = depth // LANES
    high = -(-(columns + 8) // 64) * 64
    lines = blocks * high
    parts = 2 if lines % (16 * length) == 0 else 1
    n1, n2, n3 = (lines // parts // k for k in (CORES, CORES * CHIPS, length))
    vmem = lambda *shape: pltpu.VMEM(shape, F32)
    half = lambda *shape: pltpu.VMEM(shape, BF16)
    here = pl.BlockSpec(memory_space=pltpu.VMEM)
    count = 2 * CHIPS + 2 * planes + 1
    output, grad_values, grad_tokens, grad_weight, grad_heads = pl.pallas_call(
        partial(layer_kernel, length, head_count),
        out_shape=(
            jax.ShapeDtypeStruct(values.shape, BF16),
            jax.ShapeDtypeStruct(values.shape, BF16),
            jax.ShapeDtypeStruct(tokens.shape, BF16),
            jax.ShapeDtypeStruct((columns, depth), F32),
            jax.ShapeDtypeStruct((8, LANES), F32),
        ),
        in_specs=[here] * 6 + [pl.BlockSpec(memory_space=pltpu.SMEM), here],
        out_specs=(here,) * 5,
        scratch_shapes=[
            vmem(pairs, tall, LANES),
            vmem(pairs, 2 * state, LANES),
            vmem(STREAMS, CORES, mid, tall, LANES),
            vmem(STREAMS, mid, tall, LANES),
            vmem(STREAMS, CHIPS, low, tall, LANES),
            vmem(STREAMS, low, tall, LANES),
            vmem(STREAMS, planes - 1, low, state + 8, LANES),
            vmem(STREAMS, planes - 1, low, state + 8, LANES),
            vmem(STREAMS, low, 2 * state, LANES),
            vmem(STREAMS, CHIPS, low, 2 * state, LANES),
            vmem(STREAMS, mid, 2 * state, LANES),
            vmem(STREAMS, mid, 2 * state, LANES),
            pltpu.SemaphoreType.DMA((STREAMS, count)),
            pltpu.SemaphoreType.DMA((STREAMS, count)),
            pltpu.SemaphoreType.DMA((STREAMS, 3)),
            vmem(lines, LANES),
            vmem(lines, LANES),
            vmem(parts, n1, LANES),
            vmem(parts, n1, LANES),
            vmem(parts, CHIPS - 1, n2, LANES),
            vmem(parts, n2, LANES),
            vmem(parts, planes - 1, n3, LANES),
            pltpu.SemaphoreType.DMA((parts, count)),
            pltpu.SemaphoreType.DMA((parts, count)),
            vmem(row_count, row_count),
            vmem(row_count, row_count),
            vmem(row_count, row_count),
            vmem(row_count, inner),
            vmem(row_count, inner),
            half(row_count, LANES),
            half(row_count, LANES),
            half(row_count, LANES),
            half(row_count, LANES),
            vmem(LANES, row_count),
            half(row_count, state),
            half(row_count, state),
            vmem(4, row_count, LANES),
            vmem(2, row_count, state),
            vmem(8, LANES),
        ],
        compiler_params=pltpu.CompilerParams(
            collective_id=0, has_side_effects=True, vmem_limit_bytes=56 << 20
        ),
    )(
        tokens, values, in_weight.T, step_bias[None], decay_log[None], skip_gain[None],
        trace_lengths, output_grad,
    )
    return output, grad_values, grad_tokens, grad_weight.T, grad_heads[:3, :head_count]


def solution(mesh):
    in_specs = (
        P(("groups", "seq"), None),
        P(("groups", "seq"), None),
        P(),
        P(),
        P(),
        P(),
        P("groups"),
        P(("groups", "seq"), None),
    )
    out_specs = (
        P(("groups", "seq"), None),
        P(("groups", "seq"), None),
        P(("groups", "seq"), None),
        P("groups", None),
        P("groups", None),
    )
    return jax.shard_map(shards, mesh=mesh, in_specs=in_specs, out_specs=out_specs, check_vma=False)
```

```python
from functools import partial

import jax
import jax.numpy as jnp
from jax import lax
from jax.experimental import pallas as pl
from jax.experimental.pallas import tpu as pltpu
from jax.sharding import PartitionSpec as P


MESH = pl.DeviceIdType.MESH
CORES = 2
CHIPS = 4


def placing(length):
    here = lax.axis_index("seq")
    core = lax.rem(here, CORES)
    chip = lax.rem(lax.div(here, CORES), CHIPS)
    plane = lax.div(here, CORES * CHIPS)
    return core, chip, plane, length // (CORES * CHIPS)


def device_at(plane, chip, core):
    return {"seq": (plane * CHIPS + chip) * CORES + core}


def greet(length):
    core, chip, plane, planes = placing(length)
    barrier = pltpu.get_barrier_semaphore()
    others = [device_at(plane, chip, 1 - core)]
    others += [device_at(plane, lax.rem(chip + d, CHIPS), core) for d in range(1, CHIPS)]
    others += [device_at(lax.rem(plane + d, planes), chip, core) for d in range(1, planes)]
    for other in others:
        pl.semaphore_signal(barrier, inc=1, device_id=other, device_id_type=MESH)
    return lambda: pl.semaphore_wait(barrier, len(others))


def sending(src, dst, send, recv, at, to):
    return pltpu.make_async_remote_copy(
        src_ref=src,
        dst_ref=dst,
        send_sem=send.at[at],
        recv_sem=recv.at[at],
        device_id=to,
        device_id_type=MESH,
    )


def scan_stream(width, places, own, out, pair, half, quad, part, zf, zb, gate, back, held, away,
                send, recv, keep):
    core, chip, plane, planes = places
    w = width
    heads = own.shape[0]
    mid, low = heads // CORES, heads // (CORES * CHIPS)
    partner = device_at(plane, chip, 1 - core)
    pending = []

    def begin(cp):
        cp.start()
        pending.append(cp)

    def settle():
        for cp in pending:
            cp.wait()
        pending.clear()

    begin(sending(own.at[pl.ds((1 - core) * mid, mid)], pair.at[core], send, recv, 0, partner))
    yield
    mine = pltpu.make_async_copy(own.at[pl.ds(core * mid, mid)], pair.at[core], keep.at[0])
    mine.start()
    mine.wait()
    yield
    settle()

    def join(h, _):
        r0, r1 = pair[0, h, w : w + 8], pair[1, h, w : w + 8]
        half[h, 0:w] = pair[1, h, 0:w] + r1[0:1] * pair[0, h, 0:w]
        half[h, w : w + 8] = r0 * r1
        half[h, w + 8 :] = pair[0, h, w + 8 :] + r0[0:1] * pair[1, h, w + 8 :]
        return 0

    lax.fori_loop(0, mid, join, 0)
    chips = [lax.rem(chip + d, CHIPS) for d in range(1, CHIPS)]
    for d, to in enumerate(chips):
        begin(
            sending(
                half.at[pl.ds(to * low, low)], quad.at[chip], send, recv, 1 + d,
                device_at(plane, to, core),
            )
        )
    mine = pltpu.make_async_copy(half.at[pl.ds(chip * low, low)], quad.at[chip], keep.at[1])
    mine.start()
    mine.wait()
    yield
    settle()

    def total(h, _):
        f, r = quad[0, h, 0:w], quad[0, h, w : w + 8]
        a = quad[CHIPS - 1, h, w + 8 :]
        for c in range(1, CHIPS):
            rc = quad[c, h, w : w + 8]
            f = quad[c, h, 0:w] + rc[0:1] * f
            r = r * rc
            e = CHIPS - 1 - c
            a = quad[e, h, w + 8 :] + quad[e, h, w : w + 1] * a
        part[h, 0:w] = f
        part[h, w : w + 8] = r
        part[h, w + 8 :] = a
        gate[h] = jnp.zeros((2 * w, gate.shape[2]), jnp.float32)
        return 0

    lax.fori_loop(0, low, total, 0)
    ups, downs = [], []
    for d in range(1, planes):
        up = sending(
            part.at[:, 0 : w + 8], zf.at[d - 1], send, recv, CHIPS + d,
            device_at(lax.rem(plane + d, planes), chip, core),
        )
        down = sending(
            part.at[:, w : 2 * w + 8], zb.at[d - 1], send, recv, CHIPS + planes + d,
            device_at(lax.rem(plane + planes - d, planes), chip, core),
        )
        pl.when(plane + d < planes)(up.start)
        pl.when(plane - d >= 0)(down.start)
        ups.append(up)
        downs.append(down)
    yield
    for d in range(planes - 1, 0, -1):

        @pl.when(plane - d >= 0)
        def _():
            ups[d - 1].wait_recv()

            def add(h, _):
                gate[h, 0:w] = zf[d - 1, h, 0:w] + zf[d - 1, h, w : w + 1] * gate[h, 0:w]
                return 0

            lax.fori_loop(0, low, add, 0)

        @pl.when(plane + d < planes)
        def _():
            downs[d - 1].wait_recv()

            def add(h, _):
                gate[h, w:] = zb[d - 1, h, 8:] + zb[d - 1, h, 0:1] * gate[h, w:]
                return 0

            lax.fori_loop(0, low, add, 0)

    def spread(h, _):
        f, a = gate[h, 0:w], gate[h, w:]
        for c in range(CHIPS):
            e = CHIPS - 1 - c
            back[c, h, 0:w] = f
            back[e, h, w:] = a
            if c < CHIPS - 1:
                f = quad[c, h, 0:w] + quad[c, h, w : w + 1] * f
                a = quad[e, h, w + 8 :] + quad[e, h, w : w + 1] * a
        return 0

    lax.fori_loop(0, low, spread, 0)
    base = CHIPS + 2 * planes
    for d, to in enumerate(chips):
        begin(
            sending(
                back.at[to], held.at[pl.ds(chip * low, low)], send, recv, base + d,
                device_at(plane, to, core),
            )
        )
    mine = pltpu.make_async_copy(back.at[chip], held.at[pl.ds(chip * low, low)], keep.at[2])
    mine.start()
    mine.wait()
    yield
    settle()

    def last(h, _):
        f, a = held[h, 0:w], held[h, w:]
        f1 = pair[0, h, 0:w] + pair[0, h, w : w + 1] * f
        a0 = pair[1, h, w + 8 :] + pair[1, h, w : w + 1] * a
        early = core == 0
        away[h, 0:w] = jnp.where(early, f1, f)
        away[h, w:] = jnp.where(early, a, a0)
        out[core * mid + h, 0:w] = jnp.where(early, f, f1)
        out[core * mid + h, w:] = jnp.where(early, a0, a)
        return 0

    lax.fori_loop(0, mid, last, 0)
    begin(sending(away, out.at[pl.ds((core) * mid, mid)], send, recv, base + CHIPS, partner))
    for d in range(1, planes):
        pl.when(plane + d < planes)(ups[d - 1].wait_send)
        pl.when(plane - d >= 0)(downs[d - 1].wait_send)
    yield
    settle()
    yield


def sum_stream(length, places, own, out, pair, half, quad, part, deep, send, recv):
    core, chip, plane, planes = places
    rows = own.shape[0]
    n1, n2, n3 = rows // CORES, rows // (CORES * CHIPS), rows // length
    partner = device_at(plane, chip, 1 - core)
    pending = []

    def begin(src, dst, at, to):
        cp = sending(src, dst, send, recv, at, to)
        cp.start()
        pending.append(cp)

    def settle():
        for cp in pending:
            cp.wait()
        pending.clear()

    begin(own.at[pl.ds((1 - core) * n1, n1)], pair, 0, partner)
    yield
    settle()
    half[...] = own[pl.ds(core * n1, n1)] + pair[...]
    chips = [lax.rem(chip + d, CHIPS) for d in range(1, CHIPS)]
    for d, to in enumerate(chips):
        begin(half.at[pl.ds(to * n2, n2)], quad.at[d], 1 + d, device_at(plane, to, core))
    yield
    settle()
    summed = half[pl.ds(chip * n2, n2)]
    for d in range(CHIPS - 1):
        summed = summed + quad[d]
    part[...] = summed
    others = [lax.rem(plane + d, planes) for d in range(1, planes)]
    for d, to in enumerate(others):
        begin(part.at[pl.ds(to * n3, n3)], deep.at[d], CHIPS + d, device_at(to, chip, core))
    yield
    settle()
    summed = part[pl.ds(plane * n3, n3)]
    for d in range(planes - 1):
        summed = summed + deep[d]
    at = core * n1 + chip * n2
    out[pl.ds(at + plane * n3, n3)] = summed
    base = CHIPS + planes
    block = out.at[pl.ds(at + plane * n3, n3)]
    for d, to in enumerate(others):
        begin(block, block, base + d, device_at(to, chip, core))
    yield
    settle()
    block = out.at[pl.ds(at, n2)]
    base += planes
    for d, to in enumerate(chips):
        begin(block, block, base + d, device_at(plane, to, core))
    yield
    settle()
    block = out.at[pl.ds(core * n1, n1)]
    begin(block, block, base + CHIPS, partner)
    yield
    settle()
    yield


F32, BF16 = jnp.float32, jnp.bfloat16
LANES = 128
FAR = -1e30
STREAMS = 2
SHARES = ((2, 3), (2, 3), (2, 4))


def dot(a, b, dims=((1,), (0,)), precision=None):
    return lax.dot_general(
        a, b, (dims, ((), ())), preferred_element_type=F32, precision=precision
    )


def thirds(x, heads):
    high = x.astype(BF16)
    rest = x - high.astype(F32)
    mid = rest.astype(BF16)
    low = (rest - mid.astype(F32)).astype(BF16)
    keep = [part.astype(F32)[:, :heads] for part in (high, mid, low)]
    keep.append(jnp.zeros((x.shape[0], LANES - 3 * heads), F32))
    return jnp.concatenate(keep, axis=1).astype(BF16)


def layer_kernel(
    length, heads, tokens, values, weight, bias, decay_log, skip_gain, lengths, grad,
    output, grad_values, grad_tokens, grad_weight, grad_heads,
    own, states, pair, half, quad, part, zf, zb, gate, back, held, away, send, recv, keep,
    stack, total, s_pair, s_half, s_quad, s_part, s_deep, s_send, s_recv,
    scores, hidden, grad_scores, mixed, mixed_back, decays3, steps3, rows3, tails3, decays_t,
    b_map, c_map, sums, grad_maps, grad_gate,
):
    ready = greet(length)
    rows, inner = values.shape
    width = inner // heads
    state = (weight.shape[0] - heads) // 2
    pairs = inner // LANES
    per = LANES // width
    here = lax.axis_index("seq")
    first_row = here * rows

    down = lax.broadcasted_iota(jnp.int32, (rows, rows), 0)
    along = lax.broadcasted_iota(jnp.int32, (rows, rows), 1)
    at = first_row + lax.broadcasted_iota(jnp.int32, (rows, 1), 0)
    at_row = first_row + lax.broadcasted_iota(jnp.int32, (1, rows), 1)
    zero = jnp.zeros((rows, 1), jnp.int32)
    trace, trace_row, prior, final = (zero.astype(F32), jnp.zeros((1, rows), F32), zero.astype(F32), zero.astype(F32))
    end = 0
    for k in range(lengths.shape[0]):
        end = end + lengths[k]
        trace += jnp.where(at >= end, 1.0, 0.0)
        trace_row += jnp.where(at_row >= end, 1.0, 0.0)
        prior += jnp.where(zero + (first_row - 1) >= end, 1.0, 0.0)
        final += jnp.where(zero + (first_row + rows - 1) >= end, 1.0, 0.0)
    carrying = jnp.where(trace == prior, 1.0, 0.0)
    tail = jnp.where(trace == final, 1.0, 0.0)
    hidden[...] = jnp.where(down >= along, jnp.where(trace == trace_row, 0.0, FAR), FAR)
    lower = jnp.where(down >= along, 1.0, 0.0).astype(F32)

    projected = dot(tokens[...], weight[...], ((1,), (1,)))
    b = projected[:, :state].astype(BF16)
    c = projected[:, state : 2 * state].astype(BF16)
    b_map[...] = b
    c_map[...] = c
    fill = jnp.zeros((1, LANES - heads), F32)
    widen = lambda x: jnp.concatenate([x, jnp.broadcast_to(fill, (x.shape[0], LANES - heads))], axis=1)
    rate = widen(-jnp.exp(decay_log[...]))
    drive = widen(projected[:, 2 * state :] + bias[...])
    steps = jnp.maximum(drive, 0.0) + jnp.log1p(jnp.exp(-jnp.abs(drive)))
    decays = dot(lower, rate * steps, precision=lax.Precision.HIGHEST)
    last = decays[rows - 1 : rows]
    end_gap = jnp.exp(last - decays) * tail
    tails = end_gap * steps
    retained = jnp.exp(last) * carrying[rows - 1 : rows]
    scores[...] = dot(c, b, ((1,), (1,)))
    decays3[...] = thirds(decays, heads)
    steps3[...] = thirds(steps, heads)
    rows3[...] = thirds(jnp.exp(decays) * carrying, heads)
    tails3[...] = thirds(tails, heads)
    decays_t[...] = decays.T
    retained3 = thirds(jnp.broadcast_to(retained, (8, LANES)), heads)
    skip3 = thirds(jnp.broadcast_to(widen(skip_gain[...]), (8, LANES)), heads)
    b_t = b.astype(F32).T.astype(BF16)
    c_t = c.astype(F32).T.astype(BF16)

    up = lax.broadcasted_iota(jnp.int32, (LANES, LANES), 0)
    lane = lax.broadcasted_iota(jnp.int32, (LANES, LANES), 1)

    def spreading(i):
        return jnp.where((up % heads == per * i + lane // width) & (up < 3 * heads), 1.0, 0.0).astype(BF16)

    def columns(i):
        return pl.ds(pl.multiple_of(i * LANES, LANES), LANES)

    def prepare(i, _):
        hot = spreading(i)
        v = values[:, columns(i)].astype(F32)
        g = grad[:, columns(i)].astype(F32)
        w = (v * dot(tails3[...], hot)).astype(BF16)
        u = (g * dot(rows3[...], hot)).astype(BF16)
        own[i, 0:state] = dot(b_t, w)
        own[i, state : state + 8] = dot(retained3, hot)
        own[i, state + 8 :] = dot(c_t, u)
        return 0

    grad_scores[...] = jnp.zeros((rows, rows), F32)
    head_up = lax.broadcasted_iota(jnp.int32, (LANES, rows), 0)
    left = lax.broadcasted_iota(jnp.int32, (1, LANES), 1) // width

    def inside(i, _):
        v = values[:, columns(i)].astype(F32)
        g = grad[:, columns(i)]
        g_t = g.astype(F32).T.astype(BF16)
        scaled = v * dot(steps3[...], spreading(i))
        y = jnp.zeros((rows, LANES), F32)
        zs = []
        for e in range(per):
            h = per * i + e
            hot = jnp.where((head_up % heads == h) & (head_up < 3 * heads), 1.0, 0.0).astype(BF16)
            fade = jnp.exp(dot(decays3[...], hot) - decays_t[pl.ds(h, 1), :] + hidden[...])
            mixing = (scores[...] * fade).astype(BF16)
            one = jnp.where(left == e, scaled, 0.0).astype(BF16)
            grad_scores[...] += dot(g, one, ((1,), (1,))) * fade
            y = y + dot(mixing, one)
            zs.append(dot(g_t[e * width : (e + 1) * width], mixing))
        mixed[:, columns(i)] = y
        mixed_back[:, columns(i)] = jnp.concatenate(zs, axis=0).T
        return 0

    places = placing(length)
    core = places[0]
    chunk = pairs // STREAMS
    mid = chunk // CORES
    done = 0

    def meanwhile(amount):
        nonlocal done
        upto = min(pairs, done + amount)
        lax.fori_loop(done, upto, inside, 0)
        done = upto

    streams = [
        scan_stream(
            state, places, own.at[pl.ds(q * chunk, chunk)], states.at[pl.ds(q * chunk, chunk)],
            *(ref.at[q] for ref in (pair, half, quad, part, zf, zb, gate, back, held, away)),
            send.at[q], recv.at[q], keep.at[q],
        )
        for q in range(STREAMS)
    ]
    for q in range(STREAMS):
        theirs = q * chunk + (1 - core) * mid
        lax.fori_loop(0, mid, lambda h, _: prepare(theirs + h, 0), 0, unroll=2)
        if q == 0:
            ready()
        next(streams[q])
        ours = q * chunk + core * mid
        lax.fori_loop(0, mid, lambda h, _: prepare(ours + h, 0), 0, unroll=2)
        next(streams[q])
    for shares in SHARES:
        for q in range(STREAMS):
            next(streams[q])
            meanwhile(shares[q] * pairs // 16)
    meanwhile(pairs)
    for q in range(STREAMS):
        next(streams[q])

    sums[...] = jnp.zeros(sums.shape, F32)
    grad_maps[...] = jnp.zeros(grad_maps.shape, F32)
    grad_gate[...] = jnp.zeros(grad_gate.shape, F32)
    tall = lax.broadcasted_iota(jnp.int32, (2 * LANES, LANES), 0)
    wide = lax.broadcasted_iota(jnp.int32, (2 * LANES, LANES), 1)

    def finish(i, _):
        hot = spreading(i)
        gather = jnp.where(wide == per * i + (tall % LANES) // width, 1.0, 0.0).astype(BF16)

        def by_head(x):
            high = x.astype(BF16)
            low = (x - high.astype(F32)).astype(BF16)
            return dot(jnp.concatenate([high, low], axis=1), gather)

        entering, adjoint = states[i, 0:state], states[i, state:]
        grad_gate[...] += by_head(
            jnp.broadcast_to(jnp.sum(entering * adjoint, axis=0, keepdims=True), (8, LANES))
        )
        entering, adjoint = entering.astype(BF16), adjoint.astype(BF16)
        v = values[:, columns(i)].astype(F32)
        g = grad[:, columns(i)].astype(F32)
        step, row, end = (dot(ref[...], hot) for ref in (steps3, rows3, tails3))
        skip = dot(skip3, hot)[0:1]
        carried = dot(c_map[...], entering) * row
        grad_weighted = dot(b_map[...], adjoint)
        y, z = mixed[:, columns(i)], mixed_back[:, columns(i)]
        weighted = v * end
        output[:, columns(i)] = (y + carried + skip * v).astype(BF16)
        grad_values[:, columns(i)] = (step * z + skip * g + grad_weighted * end).astype(BF16)
        grad_maps[0] += dot(weighted.astype(BF16), adjoint, ((1,), (1,)))
        grad_maps[1] += dot((g * row).astype(BF16), entering, ((1,), (1,)))
        scaled = (v * step).astype(BF16).astype(F32)
        sums[0] += by_head(g * (y + carried) - scaled * z - weighted * grad_weighted)
        sums[1] += by_head(v * z)
        sums[2] += by_head(v * grad_weighted)
        sums[3] += by_head(g * v)
        return 0

    for q in range(STREAMS):
        ours = q * chunk + core * mid
        lax.fori_loop(0, mid, lambda h, _: finish(ours + h, 0), 0, unroll=2)
        next(streams[q])
        theirs = q * chunk + (1 - core) * mid
        lax.fori_loop(0, mid, lambda h, _: finish(theirs + h, 0), 0, unroll=2)
    through = sums[2]
    grad_last = jnp.sum(tails * through, axis=0, keepdims=True) + retained * grad_gate[0:1]
    grad_rates = dot(lower, sums[0], ((0,), (0,)), lax.Precision.HIGHEST) + grad_last
    grad_steps = sums[1] + end_gap * through + rate * grad_rates
    grad_drive = grad_steps * jax.nn.sigmoid(drive)
    grad_s = grad_scores[...]
    grad_b = grad_maps[0] + dot(grad_s.T.astype(BF16), c)
    grad_c = grad_maps[1] + dot(grad_s.astype(BF16), b)
    grad_maps_b = jnp.concatenate([grad_b, grad_c], axis=1)
    rounded = grad_maps_b.astype(BF16)
    rounded_drive = grad_drive[:, :heads].astype(BF16)
    split = 2 * state
    flipped = jnp.concatenate([grad_maps_b.T, grad_drive.T[:heads]], axis=0).astype(BF16)
    blocks = tokens.shape[1] // LANES
    high, used = stack.shape[0] // blocks, split + heads
    stack[used : high] = jnp.zeros((high - used, LANES), F32)
    stack[used : used + 1] = jnp.sum(grad_drive, axis=0, keepdims=True)
    stack[used + 1 : used + 2] = rate * jnp.sum(
        grad_rates * steps, axis=0, keepdims=True
    )
    stack[used + 2 : used + 3] = jnp.sum(sums[3], axis=0, keepdims=True)

    def fill(k):
        base = k * high
        stack[base : base + used] = dot(flipped, tokens[:, k * LANES : (k + 1) * LANES])
        if k:
            stack[base + used : base + high] = jnp.zeros((high - used, LANES), F32)

    split_rows = stack.shape[0] // s_pair.shape[0]
    streams = [
        sum_stream(
            length, places, stack.at[pl.ds(q * split_rows, split_rows)],
            total.at[pl.ds(q * split_rows, split_rows)],
            *(ref.at[q] for ref in (s_pair, s_half, s_quad, s_part, s_deep, s_send, s_recv)),
        )
        for q in range(s_pair.shape[0])
    ]
    filled = 0
    for q, stream in enumerate(streams):
        while filled < blocks and filled * high < (q + 1) * split_rows:
            fill(filled)
            filled += 1
        next(stream)
    grad_tokens[...] = (
        dot(rounded, weight[:split])
        + dot(rounded_drive, weight[split:])
    ).astype(BF16)
    for _ in range(6):
        for stream in streams:
            next(stream)
    for k in range(blocks):
        grad_weight[:, k * LANES : (k + 1) * LANES] = total[k * high : k * high + used]
    grad_heads[...] = total[used : used + 8]


def shards(tokens, values, in_weight, step_bias, decay_log, skip_gain, trace_lengths, output_grad):
    row_count, inner = values.shape
    depth = tokens.shape[1]
    head_count = step_bias.shape[0]
    columns = in_weight.shape[1]
    state = (columns - head_count) // 2
    length = lax.axis_size("seq")
    planes = length // (CORES * CHIPS)
    pairs = inner // LANES
    chunk = pairs // STREAMS
    mid, low = chunk // CORES, chunk // (CORES * CHIPS)
    tall = 2 * state + 8
    blocks = depth // LANES
    high = -(-(columns + 8) // 64) * 64
    lines = blocks * high
    parts = 2 if lines % (16 * length) == 0 else 1
    n1, n2, n3 = (lines // parts // k for k in (CORES, CORES * CHIPS, length))
    vmem = lambda *shape: pltpu.VMEM(shape, F32)
    half = lambda *shape: pltpu.VMEM(shape, BF16)
    here = pl.BlockSpec(memory_space=pltpu.VMEM)
    count = 2 * CHIPS + 2 * planes + 1
    output, grad_values, grad_tokens, grad_weight, grad_heads = pl.pallas_call(
        partial(layer_kernel, length, head_count),
        out_shape=(
            jax.ShapeDtypeStruct(values.shape, BF16),
            jax.ShapeDtypeStruct(values.shape, BF16),
            jax.ShapeDtypeStruct(tokens.shape, BF16),
            jax.ShapeDtypeStruct((columns, depth), F32),
            jax.ShapeDtypeStruct((8, LANES), F32),
        ),
        in_specs=[here] * 6 + [pl.BlockSpec(memory_space=pltpu.SMEM), here],
        out_specs=(here,) * 5,
        scratch_shapes=[
            vmem(pairs, tall, LANES),
            vmem(pairs, 2 * state, LANES),
            vmem(STREAMS, CORES, mid, tall, LANES),
            vmem(STREAMS, mid, tall, LANES),
            vmem(STREAMS, CHIPS, low, tall, LANES),
            vmem(STREAMS, low, tall, LANES),
            vmem(STREAMS, planes - 1, low, state + 8, LANES),
            vmem(STREAMS, planes - 1, low, state + 8, LANES),
            vmem(STREAMS, low, 2 * state, LANES),
            vmem(STREAMS, CHIPS, low, 2 * state, LANES),
            vmem(STREAMS, mid, 2 * state, LANES),
            vmem(STREAMS, mid, 2 * state, LANES),
            pltpu.SemaphoreType.DMA((STREAMS, count)),
            pltpu.SemaphoreType.DMA((STREAMS, count)),
            pltpu.SemaphoreType.DMA((STREAMS, 3)),
            vmem(lines, LANES),
            vmem(lines, LANES),
            vmem(parts, n1, LANES),
            vmem(parts, n1, LANES),
            vmem(parts, CHIPS - 1, n2, LANES),
            vmem(parts, n2, LANES),
            vmem(parts, planes - 1, n3, LANES),
            pltpu.SemaphoreType.DMA((parts, count)),
            pltpu.SemaphoreType.DMA((parts, count)),
            vmem(row_count, row_count),
            vmem(row_count, row_count),
            vmem(row_count, row_count),
            vmem(row_count, inner),
            vmem(row_count, inner),
            half(row_count, LANES),
            half(row_count, LANES),
            half(row_count, LANES),
            half(row_count, LANES),
            vmem(LANES, row_count),
            half(row_count, state),
            half(row_count, state),
            vmem(4, row_count, LANES),
            vmem(2, row_count, state),
            vmem(8, LANES),
        ],
        compiler_params=pltpu.CompilerParams(
            collective_id=0, has_side_effects=True, vmem_limit_bytes=56 << 20
        ),
    )(
        tokens, values, in_weight.T, step_bias[None], decay_log[None], skip_gain[None],
        trace_lengths, output_grad,
    )
    return output, grad_values, grad_tokens, grad_weight.T, grad_heads[:3, :head_count]


def solution(mesh):
    in_specs = (
        P(("groups", "seq"), None),
        P(("groups", "seq"), None),
        P(),
        P(),
        P(),
        P(),
        P("groups"),
        P(("groups", "seq"), None),
    )
    out_specs = (
        P(("groups", "seq"), None),
        P(("groups", "seq"), None),
        P(("groups", "seq"), None),
        P("groups", None),
        P("groups", None),
    )
    return jax.shard_map(shards, mesh=mesh, in_specs=in_specs, out_specs=out_specs, check_vma=False)
```

```python
from functools import partial

import jax
import jax.numpy as jnp
from jax import lax
from jax.experimental import pallas as pl
from jax.experimental.pallas import tpu as pltpu
from jax.sharding import PartitionSpec as P


MESH = pl.DeviceIdType.MESH
CORES = 2
CHIPS = 4


def placing(length):
    here = lax.axis_index("seq")
    core = lax.rem(here, CORES)
    chip = lax.rem(lax.div(here, CORES), CHIPS)
    plane = lax.div(here, CORES * CHIPS)
    return core, chip, plane, length // (CORES * CHIPS)


def device_at(plane, chip, core):
    return {"seq": (plane * CHIPS + chip) * CORES + core}


def greet(length):
    core, chip, plane, planes = placing(length)
    barrier = pltpu.get_barrier_semaphore()
    others = [device_at(plane, chip, 1 - core)]
    others += [device_at(plane, lax.rem(chip + d, CHIPS), core) for d in range(1, CHIPS)]
    others += [device_at(lax.rem(plane + d, planes), chip, core) for d in range(1, planes)]
    for other in others:
        pl.semaphore_signal(barrier, inc=1, device_id=other, device_id_type=MESH)
    return lambda: pl.semaphore_wait(barrier, len(others))


def sending(src, dst, send, recv, at, to):
    return pltpu.make_async_remote_copy(
        src_ref=src,
        dst_ref=dst,
        send_sem=send.at[at],
        recv_sem=recv.at[at],
        device_id=to,
        device_id_type=MESH,
    )


def scan_stream(width, places, own, out, pair, half, quad, part, zf, zb, gate, back, held, away,
                send, recv, keep):
    core, chip, plane, planes = places
    w = width
    heads = own.shape[0]
    mid, low = heads // CORES, heads // (CORES * CHIPS)
    partner = device_at(plane, chip, 1 - core)
    pending = []

    def begin(cp):
        cp.start()
        pending.append(cp)

    def settle():
        for cp in pending:
            cp.wait()
        pending.clear()

    begin(sending(own.at[pl.ds((1 - core) * mid, mid)], pair.at[core], send, recv, 0, partner))
    yield
    mine = pltpu.make_async_copy(own.at[pl.ds(core * mid, mid)], pair.at[core], keep.at[0])
    mine.start()
    mine.wait()
    yield
    settle()

    def join(h, _):
        r0, r1 = pair[0, h, w : w + 8], pair[1, h, w : w + 8]
        half[h, 0:w] = pair[1, h, 0:w] + r1[0:1] * pair[0, h, 0:w]
        half[h, w : w + 8] = r0 * r1
        half[h, w + 8 :] = pair[0, h, w + 8 :] + r0[0:1] * pair[1, h, w + 8 :]
        return 0

    lax.fori_loop(0, mid, join, 0)
    chips = [lax.rem(chip + d, CHIPS) for d in range(1, CHIPS)]
    for d, to in enumerate(chips):
        begin(
            sending(
                half.at[pl.ds(to * low, low)], quad.at[chip], send, recv, 1 + d,
                device_at(plane, to, core),
            )
        )
    mine = pltpu.make_async_copy(half.at[pl.ds(chip * low, low)], quad.at[chip], keep.at[1])
    mine.start()
    mine.wait()
    yield
    settle()

    def total(h, _):
        f, r = quad[0, h, 0:w], quad[0, h, w : w + 8]
        a = quad[CHIPS - 1, h, w + 8 :]
        for c in range(1, CHIPS):
            rc = quad[c, h, w : w + 8]
            f = quad[c, h, 0:w] + rc[0:1] * f
            r = r * rc
            e = CHIPS - 1 - c
            a = quad[e, h, w + 8 :] + quad[e, h, w : w + 1] * a
        part[h, 0:w] = f
        part[h, w : w + 8] = r
        part[h, w + 8 :] = a
        gate[h] = jnp.zeros((2 * w, gate.shape[2]), jnp.float32)
        return 0

    lax.fori_loop(0, low, total, 0)
    ups, downs = [], []
    for d in range(1, planes):
        up = sending(
            part.at[:, 0 : w + 8], zf.at[d - 1], send, recv, CHIPS + d,
            device_at(lax.rem(plane + d, planes), chip, core),
        )
        down = sending(
            part.at[:, w : 2 * w + 8], zb.at[d - 1], send, recv, CHIPS + planes + d,
            device_at(lax.rem(plane + planes - d, planes), chip, core),
        )
        pl.when(plane + d < planes)(up.start)
        pl.when(plane - d >= 0)(down.start)
        ups.append(up)
        downs.append(down)
    yield
    for d in range(planes - 1, 0, -1):

        @pl.when(plane - d >= 0)
        def _():
            ups[d - 1].wait_recv()

            def add(h, _):
                gate[h, 0:w] = zf[d - 1, h, 0:w] + zf[d - 1, h, w : w + 1] * gate[h, 0:w]
                return 0

            lax.fori_loop(0, low, add, 0)

        @pl.when(plane + d < planes)
        def _():
            downs[d - 1].wait_recv()

            def add(h, _):
                gate[h, w:] = zb[d - 1, h, 8:] + zb[d - 1, h, 0:1] * gate[h, w:]
                return 0

            lax.fori_loop(0, low, add, 0)

    def spread(h, _):
        f, a = gate[h, 0:w], gate[h, w:]
        for c in range(CHIPS):
            e = CHIPS - 1 - c
            back[c, h, 0:w] = f
            back[e, h, w:] = a
            if c < CHIPS - 1:
                f = quad[c, h, 0:w] + quad[c, h, w : w + 1] * f
                a = quad[e, h, w + 8 :] + quad[e, h, w : w + 1] * a
        return 0

    lax.fori_loop(0, low, spread, 0)
    base = CHIPS + 2 * planes
    for d, to in enumerate(chips):
        begin(
            sending(
                back.at[to], held.at[pl.ds(chip * low, low)], send, recv, base + d,
                device_at(plane, to, core),
            )
        )
    mine = pltpu.make_async_copy(back.at[chip], held.at[pl.ds(chip * low, low)], keep.at[2])
    mine.start()
    mine.wait()
    yield
    settle()

    def last(h, _):
        f, a = held[h, 0:w], held[h, w:]
        f1 = pair[0, h, 0:w] + pair[0, h, w : w + 1] * f
        a0 = pair[1, h, w + 8 :] + pair[1, h, w : w + 1] * a
        early = core == 0
        away[h, 0:w] = jnp.where(early, f1, f)
        away[h, w:] = jnp.where(early, a, a0)
        out[core * mid + h, 0:w] = jnp.where(early, f, f1)
        out[core * mid + h, w:] = jnp.where(early, a0, a)
        return 0

    lax.fori_loop(0, mid, last, 0)
    begin(sending(away, out.at[pl.ds((core) * mid, mid)], send, recv, base + CHIPS, partner))
    for d in range(1, planes):
        pl.when(plane + d < planes)(ups[d - 1].wait_send)
        pl.when(plane - d >= 0)(downs[d - 1].wait_send)
    yield
    settle()
    yield


def sum_stream(length, places, own, out, pair, half, quad, part, deep, send, recv):
    core, chip, plane, planes = places
    rows = own.shape[0]
    n1, n2, n3 = rows // CORES, rows // (CORES * CHIPS), rows // length
    partner = device_at(plane, chip, 1 - core)
    pending = []

    def begin(src, dst, at, to):
        cp = sending(src, dst, send, recv, at, to)
        cp.start()
        pending.append(cp)

    def settle():
        for cp in pending:
            cp.wait()
        pending.clear()

    begin(own.at[pl.ds((1 - core) * n1, n1)], pair, 0, partner)
    yield
    settle()
    half[...] = own[pl.ds(core * n1, n1)] + pair[...]
    chips = [lax.rem(chip + d, CHIPS) for d in range(1, CHIPS)]
    for d, to in enumerate(chips):
        begin(half.at[pl.ds(to * n2, n2)], quad.at[d], 1 + d, device_at(plane, to, core))
    yield
    settle()
    summed = half[pl.ds(chip * n2, n2)]
    for d in range(CHIPS - 1):
        summed = summed + quad[d]
    part[...] = summed
    others = [lax.rem(plane + d, planes) for d in range(1, planes)]
    for d, to in enumerate(others):
        begin(part.at[pl.ds(to * n3, n3)], deep.at[d], CHIPS + d, device_at(to, chip, core))
    yield
    settle()
    summed = part[pl.ds(plane * n3, n3)]
    for d in range(planes - 1):
        summed = summed + deep[d]
    at = core * n1 + chip * n2
    out[pl.ds(at + plane * n3, n3)] = summed
    base = CHIPS + planes
    block = out.at[pl.ds(at + plane * n3, n3)]
    for d, to in enumerate(others):
        begin(block, block, base + d, device_at(to, chip, core))
    yield
    settle()
    block = out.at[pl.ds(at, n2)]
    base += planes
    for d, to in enumerate(chips):
        begin(block, block, base + d, device_at(plane, to, core))
    yield
    settle()
    block = out.at[pl.ds(core * n1, n1)]
    begin(block, block, base + CHIPS, partner)
    yield
    settle()
    yield


F32, BF16 = jnp.float32, jnp.bfloat16
LANES = 128
FAR = -1e30
STREAMS = 2
SHARES = ((2, 3), (2, 3), (2, 4))


def dot(a, b, dims=((1,), (0,)), precision=None):
    return lax.dot_general(
        a, b, (dims, ((), ())), preferred_element_type=F32, precision=precision
    )


def thirds(x, heads):
    high = x.astype(BF16)
    rest = x - high.astype(F32)
    mid = rest.astype(BF16)
    low = (rest - mid.astype(F32)).astype(BF16)
    keep = [part.astype(F32)[:, :heads] for part in (high, mid, low)]
    keep.append(jnp.zeros((x.shape[0], LANES - 3 * heads), F32))
    return jnp.concatenate(keep, axis=1).astype(BF16)


def layer_kernel(
    length, heads, tokens, values, weight, bias, decay_log, skip_gain, lengths, grad,
    output_out, values_out, grad_tokens, grad_weight, grad_heads,
    output, grad_values, leave, own, states, pair, half, quad, part, zf, zb, gate, back, held, away, send, recv, keep,
    stack, total, s_pair, s_half, s_quad, s_part, s_deep, s_send, s_recv,
    scores, hidden, grad_scores, mixed, mixed_back, decays3, steps3, rows3, tails3, decays_t,
    b_map, c_map, sums, grad_maps, grad_gate,
):
    ready = greet(length)
    rows, inner = values.shape
    width = inner // heads
    state = (weight.shape[0] - heads) // 2
    pairs = inner // LANES
    per = LANES // width
    here = lax.axis_index("seq")
    first_row = here * rows

    down = lax.broadcasted_iota(jnp.int32, (rows, rows), 0)
    along = lax.broadcasted_iota(jnp.int32, (rows, rows), 1)
    at = first_row + lax.broadcasted_iota(jnp.int32, (rows, 1), 0)
    at_row = first_row + lax.broadcasted_iota(jnp.int32, (1, rows), 1)
    zero = jnp.zeros((rows, 1), jnp.int32)
    trace, trace_row, prior, final = (zero.astype(F32), jnp.zeros((1, rows), F32), zero.astype(F32), zero.astype(F32))
    end = 0
    for k in range(lengths.shape[0]):
        end = end + lengths[k]
        trace += jnp.where(at >= end, 1.0, 0.0)
        trace_row += jnp.where(at_row >= end, 1.0, 0.0)
        prior += jnp.where(zero + (first_row - 1) >= end, 1.0, 0.0)
        final += jnp.where(zero + (first_row + rows - 1) >= end, 1.0, 0.0)
    carrying = jnp.where(trace == prior, 1.0, 0.0)
    tail = jnp.where(trace == final, 1.0, 0.0)
    hidden[...] = jnp.where(down >= along, jnp.where(trace == trace_row, 0.0, FAR), FAR)
    lower = jnp.where(down >= along, 1.0, 0.0).astype(F32)

    projected = dot(tokens[...], weight[...], ((1,), (1,)))
    b = projected[:, :state].astype(BF16)
    c = projected[:, state : 2 * state].astype(BF16)
    b_map[...] = b
    c_map[...] = c
    fill = jnp.zeros((1, LANES - heads), F32)
    widen = lambda x: jnp.concatenate([x, jnp.broadcast_to(fill, (x.shape[0], LANES - heads))], axis=1)
    rate = widen(-jnp.exp(decay_log[...]))
    drive = widen(projected[:, 2 * state :] + bias[...])
    steps = jnp.maximum(drive, 0.0) + jnp.log1p(jnp.exp(-jnp.abs(drive)))
    decays = dot(lower, rate * steps, precision=lax.Precision.HIGHEST)
    last = decays[rows - 1 : rows]
    end_gap = jnp.exp(last - decays) * tail
    tails = end_gap * steps
    retained = jnp.exp(last) * carrying[rows - 1 : rows]
    scores[...] = dot(c, b, ((1,), (1,)))
    decays3[...] = thirds(decays, heads)
    steps3[...] = thirds(steps, heads)
    rows3[...] = thirds(jnp.exp(decays) * carrying, heads)
    tails3[...] = thirds(tails, heads)
    decays_t[...] = decays.T
    retained3 = thirds(jnp.broadcast_to(retained, (8, LANES)), heads)
    skip3 = thirds(jnp.broadcast_to(widen(skip_gain[...]), (8, LANES)), heads)
    b_t = b.astype(F32).T.astype(BF16)
    c_t = c.astype(F32).T.astype(BF16)

    up = lax.broadcasted_iota(jnp.int32, (LANES, LANES), 0)
    lane = lax.broadcasted_iota(jnp.int32, (LANES, LANES), 1)

    def spreading(i):
        return jnp.where((up % heads == per * i + lane // width) & (up < 3 * heads), 1.0, 0.0).astype(BF16)

    def columns(i):
        return pl.ds(pl.multiple_of(i * LANES, LANES), LANES)

    def prepare(i, _):
        hot = spreading(i)
        v = values[:, columns(i)].astype(F32)
        g = grad[:, columns(i)].astype(F32)
        w = (v * dot(tails3[...], hot)).astype(BF16)
        u = (g * dot(rows3[...], hot)).astype(BF16)
        own[i, 0:state] = dot(b_t, w)
        own[i, state : state + 8] = dot(retained3, hot)
        own[i, state + 8 :] = dot(c_t, u)
        return 0

    grad_scores[...] = jnp.zeros((rows, rows), F32)
    head_up = lax.broadcasted_iota(jnp.int32, (LANES, rows), 0)
    left = lax.broadcasted_iota(jnp.int32, (1, LANES), 1) // width

    def inside(i, _):
        v = values[:, columns(i)].astype(F32)
        g = grad[:, columns(i)]
        g_t = g.astype(F32).T.astype(BF16)
        scaled = v * dot(steps3[...], spreading(i))
        y = jnp.zeros((rows, LANES), F32)
        zs = []
        for e in range(per):
            h = per * i + e
            hot = jnp.where((head_up % heads == h) & (head_up < 3 * heads), 1.0, 0.0).astype(BF16)
            fade = jnp.exp(dot(decays3[...], hot) - decays_t[pl.ds(h, 1), :] + hidden[...])
            mixing = (scores[...] * fade).astype(BF16)
            one = jnp.where(left == e, scaled, 0.0).astype(BF16)
            grad_scores[...] += dot(g, one, ((1,), (1,))) * fade
            y = y + dot(mixing, one)
            zs.append(dot(g_t[e * width : (e + 1) * width], mixing))
        mixed[:, columns(i)] = y
        mixed_back[:, columns(i)] = jnp.concatenate(zs, axis=0).T
        return 0

    places = placing(length)
    core = places[0]
    chunk = pairs // STREAMS
    mid = chunk // CORES
    done = 0

    def meanwhile(amount):
        nonlocal done
        upto = min(pairs, done + amount)
        lax.fori_loop(done, upto, inside, 0)
        done = upto

    streams = [
        scan_stream(
            state, places, own.at[pl.ds(q * chunk, chunk)], states.at[pl.ds(q * chunk, chunk)],
            *(ref.at[q] for ref in (pair, half, quad, part, zf, zb, gate, back, held, away)),
            send.at[q], recv.at[q], keep.at[q],
        )
        for q in range(STREAMS)
    ]
    for q in range(STREAMS):
        theirs = q * chunk + (1 - core) * mid
        lax.fori_loop(0, mid, lambda h, _: prepare(theirs + h, 0), 0, unroll=2)
        if q == 0:
            ready()
        next(streams[q])
        ours = q * chunk + core * mid
        lax.fori_loop(0, mid, lambda h, _: prepare(ours + h, 0), 0, unroll=2)
        next(streams[q])
    for shares in SHARES:
        for q in range(STREAMS):
            next(streams[q])
            meanwhile(shares[q] * pairs // 16)
    meanwhile(pairs)
    for q in range(STREAMS):
        next(streams[q])

    sums[...] = jnp.zeros(sums.shape, F32)
    grad_maps[...] = jnp.zeros(grad_maps.shape, F32)
    grad_gate[...] = jnp.zeros(grad_gate.shape, F32)
    tall = lax.broadcasted_iota(jnp.int32, (2 * LANES, LANES), 0)
    wide = lax.broadcasted_iota(jnp.int32, (2 * LANES, LANES), 1)

    def finish(i, _):
        hot = spreading(i)
        gather = jnp.where(wide == per * i + (tall % LANES) // width, 1.0, 0.0).astype(BF16)

        def by_head(x):
            high = x.astype(BF16)
            low = (x - high.astype(F32)).astype(BF16)
            return dot(jnp.concatenate([high, low], axis=1), gather)

        entering, adjoint = states[i, 0:state], states[i, state:]
        grad_gate[...] += by_head(
            jnp.broadcast_to(jnp.sum(entering * adjoint, axis=0, keepdims=True), (8, LANES))
        )
        entering, adjoint = entering.astype(BF16), adjoint.astype(BF16)
        v = values[:, columns(i)].astype(F32)
        g = grad[:, columns(i)].astype(F32)
        step, row, end = (dot(ref[...], hot) for ref in (steps3, rows3, tails3))
        skip = dot(skip3, hot)[0:1]
        carried = dot(c_map[...], entering) * row
        grad_weighted = dot(b_map[...], adjoint)
        y, z = mixed[:, columns(i)], mixed_back[:, columns(i)]
        weighted = v * end
        output[:, columns(i)] = (y + carried + skip * v).astype(BF16)
        grad_values[:, columns(i)] = (step * z + skip * g + grad_weighted * end).astype(BF16)
        grad_maps[0] += dot(weighted.astype(BF16), adjoint, ((1,), (1,)))
        grad_maps[1] += dot((g * row).astype(BF16), entering, ((1,), (1,)))
        scaled = (v * step).astype(BF16).astype(F32)
        sums[0] += by_head(g * (y + carried) - scaled * z - weighted * grad_weighted)
        sums[1] += by_head(v * z)
        sums[2] += by_head(v * grad_weighted)
        sums[3] += by_head(g * v)
        return 0

    for q in range(STREAMS):
        ours = q * chunk + core * mid
        lax.fori_loop(0, mid, lambda h, _: finish(ours + h, 0), 0, unroll=2)
        next(streams[q])
        theirs = q * chunk + (1 - core) * mid
        lax.fori_loop(0, mid, lambda h, _: finish(theirs + h, 0), 0, unroll=2)
    leaving = [
        pltpu.make_async_copy(output, output_out, leave.at[0]),
        pltpu.make_async_copy(grad_values, values_out, leave.at[1]),
    ]
    for cp in leaving:
        cp.start()
    through = sums[2]
    grad_last = jnp.sum(tails * through, axis=0, keepdims=True) + retained * grad_gate[0:1]
    grad_rates = dot(lower, sums[0], ((0,), (0,)), lax.Precision.HIGHEST) + grad_last
    grad_steps = sums[1] + end_gap * through + rate * grad_rates
    grad_drive = grad_steps * jax.nn.sigmoid(drive)
    grad_s = grad_scores[...]
    grad_b = grad_maps[0] + dot(grad_s.T.astype(BF16), c)
    grad_c = grad_maps[1] + dot(grad_s.astype(BF16), b)
    grad_maps_b = jnp.concatenate([grad_b, grad_c], axis=1)
    rounded = grad_maps_b.astype(BF16)
    rounded_drive = grad_drive[:, :heads].astype(BF16)
    split = 2 * state
    flipped = jnp.concatenate([grad_maps_b.T, grad_drive.T[:heads]], axis=0).astype(BF16)
    blocks = tokens.shape[1] // LANES
    high, used = stack.shape[0] // blocks, split + heads
    stack[used : high] = jnp.zeros((high - used, LANES), F32)
    stack[used : used + 1] = jnp.sum(grad_drive, axis=0, keepdims=True)
    stack[used + 1 : used + 2] = rate * jnp.sum(
        grad_rates * steps, axis=0, keepdims=True
    )
    stack[used + 2 : used + 3] = jnp.sum(sums[3], axis=0, keepdims=True)

    def fill(k):
        base = k * high
        stack[base : base + used] = dot(flipped, tokens[:, k * LANES : (k + 1) * LANES])
        if k:
            stack[base + used : base + high] = jnp.zeros((high - used, LANES), F32)

    split_rows = stack.shape[0] // s_pair.shape[0]
    streams = [
        sum_stream(
            length, places, stack.at[pl.ds(q * split_rows, split_rows)],
            total.at[pl.ds(q * split_rows, split_rows)],
            *(ref.at[q] for ref in (s_pair, s_half, s_quad, s_part, s_deep, s_send, s_recv)),
        )
        for q in range(s_pair.shape[0])
    ]
    filled = 0
    for q, stream in enumerate(streams):
        while filled < blocks and filled * high < (q + 1) * split_rows:
            fill(filled)
            filled += 1
        next(stream)
    grad_tokens[...] = (
        dot(rounded, weight[:split])
        + dot(rounded_drive, weight[split:])
    ).astype(BF16)
    for _ in range(6):
        for stream in streams:
            next(stream)
    for k in range(blocks):
        grad_weight[:, k * LANES : (k + 1) * LANES] = total[k * high : k * high + used]
    grad_heads[...] = total[used : used + 8]
    for cp in leaving:
        cp.wait()


def shards(tokens, values, in_weight, step_bias, decay_log, skip_gain, trace_lengths, output_grad):
    row_count, inner = values.shape
    depth = tokens.shape[1]
    head_count = step_bias.shape[0]
    columns = in_weight.shape[1]
    state = (columns - head_count) // 2
    length = lax.axis_size("seq")
    planes = length // (CORES * CHIPS)
    pairs = inner // LANES
    chunk = pairs // STREAMS
    mid, low = chunk // CORES, chunk // (CORES * CHIPS)
    tall = 2 * state + 8
    blocks = depth // LANES
    high = -(-(columns + 8) // 64) * 64
    lines = blocks * high
    parts = 5 if lines % (40 * length) == 0 else 1
    n1, n2, n3 = (lines // parts // k for k in (CORES, CORES * CHIPS, length))
    vmem = lambda *shape: pltpu.VMEM(shape, F32)
    half = lambda *shape: pltpu.VMEM(shape, BF16)
    here = pl.BlockSpec(memory_space=pltpu.VMEM)
    count = 2 * CHIPS + 2 * planes + 1
    output, grad_values, grad_tokens, grad_weight, grad_heads = pl.pallas_call(
        partial(layer_kernel, length, head_count),
        out_shape=(
            jax.ShapeDtypeStruct(values.shape, BF16),
            jax.ShapeDtypeStruct(values.shape, BF16),
            jax.ShapeDtypeStruct(tokens.shape, BF16),
            jax.ShapeDtypeStruct((columns, depth), F32),
            jax.ShapeDtypeStruct((8, LANES), F32),
        ),
        in_specs=[here] * 6 + [pl.BlockSpec(memory_space=pltpu.SMEM), here],
        out_specs=(pl.BlockSpec(memory_space=pl.ANY),) * 2 + (here,) * 3,
        scratch_shapes=[
            half(row_count, inner),
            half(row_count, inner),
            pltpu.SemaphoreType.DMA((2,)),
            vmem(pairs, tall, LANES),
            vmem(pairs, 2 * state, LANES),
            vmem(STREAMS, CORES, mid, tall, LANES),
            vmem(STREAMS, mid, tall, LANES),
            vmem(STREAMS, CHIPS, low, tall, LANES),
            vmem(STREAMS, low, tall, LANES),
            vmem(STREAMS, planes - 1, low, state + 8, LANES),
            vmem(STREAMS, planes - 1, low, state + 8, LANES),
            vmem(STREAMS, low, 2 * state, LANES),
            vmem(STREAMS, CHIPS, low, 2 * state, LANES),
            vmem(STREAMS, mid, 2 * state, LANES),
            vmem(STREAMS, mid, 2 * state, LANES),
            pltpu.SemaphoreType.DMA((STREAMS, count)),
            pltpu.SemaphoreType.DMA((STREAMS, count)),
            pltpu.SemaphoreType.DMA((STREAMS, 3)),
            vmem(lines, LANES),
            vmem(lines, LANES),
            vmem(parts, n1, LANES),
            vmem(parts, n1, LANES),
            vmem(parts, CHIPS - 1, n2, LANES),
            vmem(parts, n2, LANES),
            vmem(parts, planes - 1, n3, LANES),
            pltpu.SemaphoreType.DMA((parts, count)),
            pltpu.SemaphoreType.DMA((parts, count)),
            vmem(row_count, row_count),
            vmem(row_count, row_count),
            vmem(row_count, row_count),
            vmem(row_count, inner),
            vmem(row_count, inner),
            half(row_count, LANES),
            half(row_count, LANES),
            half(row_count, LANES),
            half(row_count, LANES),
            vmem(LANES, row_count),
            half(row_count, state),
            half(row_count, state),
            vmem(4, row_count, LANES),
            vmem(2, row_count, state),
            vmem(8, LANES),
        ],
        compiler_params=pltpu.CompilerParams(
            collective_id=0, has_side_effects=True, vmem_limit_bytes=56 << 20
        ),
    )(
        tokens, values, in_weight.T, step_bias[None], decay_log[None], skip_gain[None],
        trace_lengths, output_grad,
    )
    return output, grad_values, grad_tokens, grad_weight.T, grad_heads[:3, :head_count]


def solution(mesh):
    in_specs = (
        P(("groups", "seq"), None),
        P(("groups", "seq"), None),
        P(),
        P(),
        P(),
        P(),
        P("groups"),
        P(("groups", "seq"), None),
    )
    out_specs = (
        P(("groups", "seq"), None),
        P(("groups", "seq"), None),
        P(("groups", "seq"), None),
        P("groups", None),
        P("groups", None),
    )
    return jax.shard_map(shards, mesh=mesh, in_specs=in_specs, out_specs=out_specs, check_vma=False)
```
